32 devices in a mesh: dev: 32 (over z, y, x, core).
Axes of the slice: x: 2, y: 2, z: 4, core: 2. Of those that a mesh axis runs over, the one named last changes fastest.
Arguments:
- tokens: bfloat16 [32768, 768], P('dev'), may hold values from -6 to 6
- seq_ids: int32 [32768], P('dev'), may hold values from 0 to 64, as said below
- cotangent: bfloat16 [32768, 768], P('dev'), may hold values from -6 to 6
- attn_gain: bfloat16 [768], P('dev'), may hold values from 0.25 to 1.75
- attn_shift: bfloat16 [768], P('dev'), may hold values from -3 to 3
- mlp_gain: bfloat16 [768], P('dev'), may hold values from 0.25 to 1.75
- mlp_shift: bfloat16 [768], P('dev'), may hold values from -3 to 3
- qkv_weight: bfloat16 [768, 2304], P('dev'), may hold values from -0.3125 to 0.3125
- qkv_bias: bfloat16 [2304], P('dev'), may hold values from -3 to 3
- out_weight: bfloat16 [768, 768], P('dev'), may hold values from -2.5 to 2.5
- out_bias: bfloat16 [768], P('dev'), may hold values from -3 to 3
- up_weight: bfloat16 [768, 3072], P('dev'), may hold values from -0.21875 to 0.21875
- up_bias: bfloat16 [3072], P('dev'), may hold values from -4 to 4
- down_weight: bfloat16 [3072, 768], P('dev'), may hold values from -0.109375 to 0.109375
- down_bias: bfloat16 [768], P('dev'), may hold values from -3 to 3
Outputs:
- block_out: bfloat16 [32768, 768], P('dev')
- grad_tokens: float32 [32768, 768], P('dev')
- grad_attn_gain: float32 [768], P('dev')
- grad_attn_shift: float32 [768], P('dev')
- grad_mlp_gain: float32 [768], P('dev')
- grad_mlp_shift: float32 [768], P('dev')
- grad_qkv_weight: float32 [768, 2304], P('dev')
- grad_qkv_bias: float32 [2304], P('dev')
- grad_out_weight: float32 [768, 768], P('dev')
- grad_out_bias: float32 [768], P('dev')
- grad_up_weight: float32 [768, 3072], P('dev')
- grad_up_bias: float32 [3072], P('dev')
- grad_down_weight: float32 [3072, 768], P('dev')
- grad_down_bias: float32 [768], P('dev')
The draws below stay inside these ranges and needn't reach their ends.
Inputs may be any that keep to these rules, and one draw needn't show every extreme that they name: seq_ids starts at 0 and rises by one at the first token of each new sequence; a sequence holds at most 1024 tokens and one holds exactly 1024; apart from token 0, the tokens of each device hold exactly two first tokens of sequences, never the device's first token, so every boundary between two devices' tokens lies inside a sequence; the later of a device's two first tokens lies at index 512 or later within the device, and on some device exactly there, so at most 512 tokens of a device continue on the next device.
All inputs are finite; a program needn't handle non-finite values.
Results may differ from the reference program's by a relative error of at most 0.012.
The reference program's roundings to bfloat16 on the way count: a program that leaves them out, or rounds other values in their place, can miss the bound.
Values may be sent and summed in bfloat16 or wider, within the bound.
No kernel may reach another device: no remote copies, remote signals or barrier semaphores. Data moves between devices by JAX's collectives and lax.ppermute only.
A program may use at most 192 MiB of HBM per device.

```python
import jax
import jax.numpy as jnp
from jax import lax

D = 768
HEADS = 12
HDIM = 64
ROT = 16
FF = 3072
TOK_DEV = 1024
TOKENS = 32768


def draw_seq_ids(key, part):
    devices = TOKENS // TOK_DEV
    midway = TOK_DEV // 2
    first_key, second_key, third_key = jax.random.split(key, 3)
    early_cut = jax.random.randint(first_key, (devices,), 1, midway)
    late_cut = jax.random.randint(second_key, (devices,), midway + 1, TOK_DEV)
    chosen = jax.random.randint(third_key, (), 1, devices)
    device_row = jnp.arange(devices)
    early_cut = jnp.where(device_row == chosen, midway, early_cut)
    late_cut = jnp.where(device_row == chosen - 1, midway, late_cut)
    column = jnp.arange(TOK_DEV)[None, :]
    cut_marks = (column == early_cut[:, None]) | (column == late_cut[:, None])
    return jnp.cumsum(cut_marks.reshape(-1).astype(jnp.int32)).astype(jnp.int32)


def block_scale(key, shape, cuts, least, top_value):
    level = 1.0
    for dim, shards_of in cuts:
        heights = jax.random.uniform(jax.random.fold_in(jax.random.fold_in(key, 6), dim), (shards_of,), jnp.float32, least / len(cuts), top_value / len(cuts))
        level = level * jnp.repeat(jnp.exp(heights), shape[dim] // shards_of).reshape((-1,) + (1,) * (len(shape) - 1 - dim))
    return level


def noise(stream_key, shape, scale, limit, cuts=(), kind=jnp.bfloat16):
    gain = block_scale(stream_key, shape, cuts, -0.22, 0.18) if cuts else 1.0
    values = jax.random.normal(stream_key, shape, jnp.float32) * scale * gain
    return jnp.minimum(jnp.maximum(values, -limit), limit).astype(kind)


def setup_inputs(seed: int = 0) -> dict:
    seeds = jax.random.split(jax.random.key(seed), 16)
    tokens = noise(seeds[0], (TOKENS, D), 1.0, 6.0, ((0, 32),))
    seq_ids = draw_seq_ids(jax.random.fold_in(seeds[15], 71), 0)
    cotangent = noise(seeds[2], (TOKENS, D), 1.0, 6.0, ((0, 32),))
    attn_gain = jnp.clip(1.0 + 0.15 * jax.random.normal(seeds[3], (D,), jnp.float32), 0.25, 1.75).astype(jnp.bfloat16)
    attn_shift = noise(seeds[4], (D,), 0.3, 3.0, ((0, 32),))
    mlp_gain = jnp.clip(1.0 + 0.15 * jax.random.normal(seeds[5], (D,), jnp.float32), 0.25, 1.75).astype(jnp.bfloat16)
    mlp_shift = noise(seeds[6], (D,), 0.3, 3.0, ((0, 32),))
    qkv_weight = noise(seeds[7], (D, 3 * D), (D // 2) ** -0.5, 0.3125, ((0, 32),))
    qkv_bias = noise(seeds[8], (3 * D,), 0.3, 3.0, ((0, 32),))
    out_weight = noise(seeds[9], (D, D), (max(8 * D // TOK_DEV, 1)) ** -0.5, 2.5, ((0, 32),))
    out_bias = noise(seeds[10], (D,), 0.3, 3.0, ((0, 32),))
    up_weight = noise(seeds[11], (D, FF), D ** -0.5, 0.21875, ((0, 32),))
    up_bias = noise(seeds[12], (FF,), 0.5, 4.0, ((0, 32),))
    down_weight = noise(seeds[13], (FF, D), FF ** -0.5, 0.109375, ((0, 32),))
    down_bias = noise(seeds[14], (D,), 0.3, 3.0, ((0, 32),))
    return dict(tokens=tokens, seq_ids=seq_ids, cotangent=cotangent, attn_gain=attn_gain, attn_shift=attn_shift, mlp_gain=mlp_gain, mlp_shift=mlp_shift, qkv_weight=qkv_weight, qkv_bias=qkv_bias, out_weight=out_weight, out_bias=out_bias, up_weight=up_weight, up_bias=up_bias, down_weight=down_weight, down_bias=down_bias)


@jax.custom_vjp
def low(v):
    return lax.optimization_barrier(v.astype(jnp.bfloat16)).astype(jnp.float32)

@jax.custom_vjp
def low_back(v):
    return v

def low_keep(v):
    return (low(v), None)

def low_pass(kept, grad):
    return (grad,)

def back_keep(v):
    return (v, None)

def back_low(kept, grad):
    return (low(grad),)
low.defvjp(low_keep, low_pass)
low_back.defvjp(back_keep, back_low)
EPSILON = 1e-05
MASKED = -1e+30
HIGHEST = lax.Precision.HIGHEST

def layer_norm(values, norm_gain, norm_shift):
    center = values - lax.optimization_barrier(jnp.mean(values, axis=-1, keepdims=True))
    spread = lax.optimization_barrier(jnp.mean(center * center, axis=-1, keepdims=True))
    return center * lax.rsqrt(spread + EPSILON) * norm_gain + norm_shift

def positions_of(seq_ids):
    row_index = jnp.arange(seq_ids.shape[0], dtype=jnp.int32)
    opening = jnp.concatenate([jnp.ones((1,), jnp.bool_), seq_ids[1:] != seq_ids[:-1]])
    seq_start = lax.cummax(jnp.where(opening, row_index, 0), axis=0)
    return row_index - seq_start

def angles_of(positions):
    frequency = 10000.0 ** (-2.0 * jnp.arange(ROT // 2, dtype=jnp.float32) / ROT)
    return positions.astype(jnp.float32)[:, None] * frequency[None, :]

def rotate(moving, angles):
    half_dims = angles.shape[-1]
    cosine = jnp.cos(angles)[:, None, :]
    sine_part = jnp.sin(angles)[:, None, :]
    first_half = moving[..., :half_dims]
    second_half = moving[..., half_dims:2 * half_dims]
    return jnp.concatenate([first_half * cosine - second_half * sine_part, second_half * cosine + first_half * sine_part, moving[..., 2 * half_dims:]], axis=-1)

def attend(query, keys, values, seq_ids):
    block_count = TOKENS // TOK_DEV
    zeros_front = jnp.zeros((TOK_DEV,) + keys.shape[1:], jnp.float32)
    padded_keys = jnp.concatenate([zeros_front, keys], axis=0)
    padded_values = jnp.concatenate([zeros_front, values], axis=0)
    padded_ids = jnp.concatenate([jnp.full((TOK_DEV,), -1, jnp.int32), seq_ids])

    def one_block(block_index):
        row_begin = (block_index * TOK_DEV).astype(jnp.int32)
        query_rows = lax.dynamic_slice_in_dim(query, row_begin, TOK_DEV, 0)
        key_rows = lax.dynamic_slice_in_dim(padded_keys, row_begin, 2 * TOK_DEV, 0)
        value_rows = lax.dynamic_slice_in_dim(padded_values, row_begin, 2 * TOK_DEV, 0)
        query_ids = lax.dynamic_slice_in_dim(seq_ids, row_begin, TOK_DEV, 0)
        key_ids = lax.dynamic_slice_in_dim(padded_ids, row_begin, 2 * TOK_DEV, 0)
        query_pos = row_begin + jnp.arange(TOK_DEV, dtype=jnp.int32)
        key_pos = row_begin - TOK_DEV + jnp.arange(2 * TOK_DEV, dtype=jnp.int32)
        allowed = (key_pos[None, :] <= query_pos[:, None]) & (key_ids[None, :] == query_ids[:, None])
        scores = low_back(jnp.einsum('qhd,khd->hqk', query_rows, key_rows, precision=HIGHEST) * HDIM ** (-0.5))
        scores = jnp.where(allowed[None], scores, MASKED)
        highest = lax.optimization_barrier(jnp.max(scores, axis=-1, keepdims=True))
        exponent = jnp.exp(scores - highest)
        attn_probs = low(exponent / lax.optimization_barrier(jnp.sum(exponent, axis=-1, keepdims=True)))
        return jnp.einsum('hqk,khd->qhd', attn_probs, value_rows, precision=HIGHEST)
    outputs = lax.map(jax.checkpoint(one_block), jnp.arange(block_count, dtype=jnp.int32))
    return outputs.reshape(TOKENS, HEADS * HDIM)

def forward(residual, gain_a, shift_a, gain_m, shift_m, w_qkv, b_qkv, w_out, b_out, w_up, b_up, w_down, b_down, seq_ids, angles):
    attn_in = low(layer_norm(residual, gain_a, shift_a))
    mixed = low_back(jnp.dot(attn_in, w_qkv, precision=HIGHEST) + b_qkv).reshape(TOKENS, 3, HEADS, HDIM)
    query = low(rotate(mixed[:, 0], angles))
    keys = low(rotate(mixed[:, 1], angles))
    values = low(mixed[:, 2])
    context = low(low_back(attend(query, keys, values, seq_ids)))
    attn_out = jnp.dot(context, w_out, precision=HIGHEST) + b_out
    mlp_in = low(layer_norm(residual, gain_m, shift_m))
    hidden = low_back(jnp.dot(mlp_in, w_up, precision=HIGHEST) + b_up)
    active = low(jax.nn.gelu(hidden, approximate=False))
    return residual + attn_out + (jnp.dot(active, w_down, precision=HIGHEST) + b_down)

def reference(tokens, seq_ids, cotangent, attn_gain, attn_shift, mlp_gain, mlp_shift, qkv_weight, qkv_bias, out_weight, out_bias, up_weight, up_bias, down_weight, down_bias):
    angles = angles_of(positions_of(seq_ids))
    params = tuple((argument.astype(jnp.float32) for argument in (attn_gain, attn_shift, mlp_gain, mlp_shift, qkv_weight, qkv_bias, out_weight, out_bias, up_weight, up_bias, down_weight, down_bias)))
    block_out, pullback = jax.vjp(lambda inputs, *weights: forward(inputs, *weights, seq_ids, angles), tokens.astype(jnp.float32), *params)
    grads = pullback(cotangent.astype(jnp.float32))
    return (block_out.astype(jnp.bfloat16), grads[0], grads[1], grads[2], grads[3], grads[4], grads[5], grads[6], grads[7], grads[8], grads[9], grads[10], grads[11], grads[12])
```

```python
import jax
import jax.numpy as jnp
from jax import lax
from jax.sharding import PartitionSpec as P

HDIM = 64
ROT = 16


EPSILON = 1e-05
MASKED = -1e30


def from_behind(value, axis, steps):
    count = lax.axis_size(axis)
    leading, last = (max(0, -steps), min(count, count - steps))
    return lax.ppermute(value, axis, [(source, source + steps) for source in range(leading, last)])


def layer_norm(values, norm_gain, norm_shift):
    center = values - jnp.mean(values, axis=-1, keepdims=True)
    spread = jnp.mean(center * center, axis=-1, keepdims=True)
    return center * lax.rsqrt(spread + EPSILON) * norm_gain + norm_shift


def angles_of(positions):
    frequency = 10000.0 ** (-2.0 * jnp.arange(ROT // 2, dtype=jnp.float32) / ROT)
    return positions.astype(jnp.float32)[:, None] * frequency[None, :]


def rotate(moving, angles):
    half_dims = angles.shape[-1]
    cosine = jnp.cos(angles)[:, None, :]
    sine_part = jnp.sin(angles)[:, None, :]
    first_half = moving[..., :half_dims]
    second_half = moving[..., half_dims : 2 * half_dims]
    return jnp.concatenate(
        [
            first_half * cosine - second_half * sine_part,
            second_half * cosine + first_half * sine_part,
            moving[..., 2 * half_dims :],
        ],
        axis=-1,
    )


def gelu_exact(values):
    return jax.nn.gelu(values, approximate=False)


def by_rows(stacked):
    return jnp.transpose(stacked, (1, 0, 2)).reshape(stacked.shape[1], -1)


def local(
    tokens,
    seq_ids,
    cotangent,
    attn_gain,
    attn_shift,
    mlp_gain,
    mlp_shift,
    qkv_weight,
    qkv_bias,
    out_weight,
    out_bias,
    up_weight,
    up_bias,
    down_weight,
    down_bias,
):
    gathered = (
        lax.all_gather(attn_gain, "dev", axis=0, tiled=True),
        lax.all_gather(attn_shift, "dev", axis=0, tiled=True),
        lax.all_gather(mlp_gain, "dev", axis=0, tiled=True),
        lax.all_gather(mlp_shift, "dev", axis=0, tiled=True),
        lax.all_gather(qkv_weight, "dev", axis=0, tiled=True),
        lax.all_gather(qkv_bias, "dev", axis=0, tiled=True),
        lax.all_gather(out_weight, "dev", axis=0, tiled=True),
        lax.all_gather(out_bias, "dev", axis=0, tiled=True),
        lax.all_gather(up_weight, "dev", axis=0, tiled=True),
        lax.all_gather(up_bias, "dev", axis=0, tiled=True),
        lax.all_gather(down_weight, "dev", axis=0, tiled=True),
        lax.all_gather(down_bias, "dev", axis=0, tiled=True),
    )
    gain_a, shift_a, gain_m, shift_m, w_qkv, b_qkv, w_out, b_out, w_up, b_up, w_down, b_down = (
        gathered
    )
    row_count = tokens.shape[0]
    model_width = tokens.shape[1]
    head_count = model_width // HDIM
    pair_count = head_count // 2
    pair_width = 2 * HDIM
    query_rows = min(512, row_count)
    score_scale = HDIM ** (-0.5)
    key_count = row_count + row_count
    row_index = jnp.arange(row_count, dtype=jnp.int32)
    prior_index = jnp.arange(row_count, dtype=jnp.int32)
    last_id = seq_ids[row_count - 1]
    trailing = jnp.sum((seq_ids == last_id).astype(jnp.int32))
    before = from_behind(jnp.stack([last_id, trailing]), "dev", 1)
    carry = jnp.where(before[0] == seq_ids[0], before[1], 0)
    seq_start = jnp.sum((seq_ids[None, :] < seq_ids[:, None]).astype(jnp.int32), axis=1)
    leading = seq_ids == seq_ids[0]
    positions = row_index - seq_start + jnp.where(leading, carry, 0)
    angles = angles_of(positions)

    def allowed_rows(offset):
        query_ids = seq_ids[offset : offset + query_rows]
        query_pos = row_index[offset : offset + query_rows]
        local_ok = (row_index[None, :] <= query_pos[:, None]) & (
            seq_ids[None, :] == query_ids[:, None]
        )
        prior_ok = leading[offset : offset + query_rows, None] & (
            prior_index[None, :] >= row_count - carry
        )
        return jnp.concatenate([prior_ok, local_ok], axis=1)

    def pair_slice(matrix, pair_index):
        return lax.dynamic_slice_in_dim(matrix, pair_index * pair_width, pair_width, 1).reshape(
            matrix.shape[0], 2, HDIM
        )

    residual = tokens.astype(jnp.float32)
    attn_in = layer_norm(residual, gain_a.astype(jnp.float32), shift_a.astype(jnp.float32)).astype(
        jnp.bfloat16
    )
    mixed = jnp.dot(attn_in, w_qkv, preferred_element_type=jnp.float32) + b_qkv.astype(jnp.float32)
    mixed = mixed.reshape(row_count, 3, head_count, HDIM)
    query = rotate(mixed[:, 0], angles).astype(jnp.bfloat16).reshape(row_count, model_width)
    own_keys = rotate(mixed[:, 1], angles).astype(jnp.bfloat16).reshape(row_count, model_width)
    own_values = mixed[:, 2].astype(jnp.bfloat16).reshape(row_count, model_width)
    prior_keys, prior_values = from_behind((own_keys, own_values), "dev", 1)
    all_keys = jnp.concatenate([prior_keys, own_keys], axis=0)
    all_values = jnp.concatenate([prior_values, own_values], axis=0)

    def pair_forward(pair_index):
        query_pair = pair_slice(query, pair_index)
        key_pair = pair_slice(all_keys, pair_index)
        value_pair = pair_slice(all_values, pair_index)
        outputs = []
        totals = []
        for offset in range(0, row_count, query_rows):
            scores = (
                jnp.einsum(
                    "qhd,khd->hqk",
                    query_pair[offset : offset + query_rows],
                    key_pair,
                    preferred_element_type=jnp.float32,
                )
                * score_scale
            )
            scores = jnp.where(allowed_rows(offset)[None], scores, MASKED)
            highest = jnp.max(scores, axis=-1, keepdims=True)
            exponent = jnp.exp(scores - highest)
            normal = jnp.sum(exponent, axis=-1, keepdims=True)
            attn_probs = (exponent / normal).astype(jnp.bfloat16)
            outputs.append(
                jnp.einsum(
                    "hqk,khd->qhd", attn_probs, value_pair, preferred_element_type=jnp.float32
                )
            )
            totals.append(highest[..., 0] + jnp.log(normal[..., 0]))
        return (
            jnp.concatenate(outputs, axis=0).reshape(row_count, pair_width),
            jnp.concatenate(totals, axis=1),
        )

    context_pairs, log_totals = lax.map(pair_forward, jnp.arange(pair_count))
    context = by_rows(context_pairs).astype(jnp.bfloat16)
    attn_out = jnp.dot(context, w_out, preferred_element_type=jnp.float32) + b_out.astype(
        jnp.float32
    )
    mlp_in = layer_norm(residual, gain_m.astype(jnp.float32), shift_m.astype(jnp.float32)).astype(
        jnp.bfloat16
    )
    ffn_parts = []
    for offset in range(0, row_count, query_rows):
        hidden = jnp.dot(
            mlp_in[offset : offset + query_rows], w_up, preferred_element_type=jnp.float32
        ) + b_up.astype(jnp.float32)
        active = gelu_exact(hidden).astype(jnp.bfloat16)
        ffn_parts.append(jnp.dot(active, w_down, preferred_element_type=jnp.float32))
    ffn_out = jnp.concatenate(ffn_parts, axis=0) + b_down.astype(jnp.float32)
    block_out = (residual + attn_out + ffn_out).astype(jnp.bfloat16)
    params = (
        lax.all_gather(attn_gain, "dev", axis=0, tiled=True),
        lax.all_gather(attn_shift, "dev", axis=0, tiled=True),
        lax.all_gather(mlp_gain, "dev", axis=0, tiled=True),
        lax.all_gather(mlp_shift, "dev", axis=0, tiled=True),
        lax.all_gather(qkv_weight, "dev", axis=0, tiled=True),
        lax.all_gather(qkv_bias, "dev", axis=0, tiled=True),
        lax.all_gather(out_weight, "dev", axis=0, tiled=True),
        lax.all_gather(out_bias, "dev", axis=0, tiled=True),
        lax.all_gather(up_weight, "dev", axis=0, tiled=True),
        lax.all_gather(up_bias, "dev", axis=0, tiled=True),
        lax.all_gather(down_weight, "dev", axis=0, tiled=True),
        lax.all_gather(down_bias, "dev", axis=0, tiled=True),
    )
    gain_a, shift_a, gain_m, shift_m, w_qkv, b_qkv, w_out, b_out, w_up, b_up, w_down, b_down = (
        params
    )
    upstream = cotangent.astype(jnp.float32)
    grad_bias_out = jnp.sum(upstream, axis=0)
    grad_w_out = jnp.einsum("td,te->de", context, cotangent, preferred_element_type=jnp.float32)
    ff_width = w_up.shape[1]
    grad_w_down = jnp.zeros((ff_width, model_width), jnp.float32)
    grad_w_up = jnp.zeros((model_width, ff_width), jnp.float32)
    grad_bias_up = jnp.zeros((ff_width,), jnp.float32)
    d_mlp_parts = []
    for offset in range(0, row_count, query_rows):
        rows_in = mlp_in[offset : offset + query_rows]
        upstream_part = cotangent[offset : offset + query_rows]
        hidden = jnp.dot(rows_in, w_up, preferred_element_type=jnp.float32) + b_up.astype(
            jnp.float32
        )
        active = gelu_exact(hidden).astype(jnp.bfloat16)
        grad_w_down = grad_w_down + jnp.einsum(
            "tf,td->fd", active, upstream_part, preferred_element_type=jnp.float32
        )
        d_active = jnp.einsum(
            "td,fd->tf", upstream_part, w_down, preferred_element_type=jnp.float32
        )
        _, gelu_pull = jax.vjp(gelu_exact, hidden)
        d_hidden = gelu_pull(d_active)[0].astype(jnp.bfloat16)
        grad_bias_up = grad_bias_up + jnp.sum(d_hidden.astype(jnp.float32), axis=0)
        grad_w_up = grad_w_up + jnp.einsum(
            "td,tf->df", rows_in, d_hidden, preferred_element_type=jnp.float32
        )
        d_mlp_parts.append(
            jnp.einsum("tf,df->td", d_hidden, w_up, preferred_element_type=jnp.float32)
        )
    d_mlp_in = jnp.concatenate(d_mlp_parts, axis=0)
    _, norm_pull_m = jax.vjp(
        layer_norm, residual, gain_m.astype(jnp.float32), shift_m.astype(jnp.float32)
    )
    d_mlp_tokens, grad_gain_m, grad_shift_m = norm_pull_m(d_mlp_in)
    d_context = jnp.einsum(
        "te,de->td", cotangent, w_out, preferred_element_type=jnp.float32
    ).astype(jnp.bfloat16)

    def pair_backward(pair_index):
        query_pair = pair_slice(query, pair_index)
        key_pair = pair_slice(all_keys, pair_index)
        value_pair = pair_slice(all_values, pair_index)
        d_pair = pair_slice(d_context, pair_index)
        total_pair = log_totals[pair_index]
        d_keys = jnp.zeros((key_count, 2, HDIM), jnp.float32)
        d_values = jnp.zeros((key_count, 2, HDIM), jnp.float32)
        d_query_parts = []
        for offset in range(0, row_count, query_rows):
            query_block = query_pair[offset : offset + query_rows]
            d_block = d_pair[offset : offset + query_rows]
            scores = (
                jnp.einsum(
                    "qhd,khd->hqk", query_block, key_pair, preferred_element_type=jnp.float32
                )
                * score_scale
            )
            scores = jnp.where(allowed_rows(offset)[None], scores, MASKED)
            prob_full = jnp.exp(scores - total_pair[:, offset : offset + query_rows, None])
            d_values = d_values + jnp.einsum(
                "hqk,qhd->khd",
                prob_full.astype(jnp.bfloat16),
                d_block,
                preferred_element_type=jnp.float32,
            )
            d_probs = jnp.einsum(
                "qhd,khd->hqk", d_block, value_pair, preferred_element_type=jnp.float32
            )
            inner = jnp.sum(prob_full * d_probs, axis=-1, keepdims=True)
            d_scores = (prob_full * (d_probs - inner)).astype(jnp.bfloat16)
            d_query_parts.append(
                jnp.einsum("hqk,khd->qhd", d_scores, key_pair, preferred_element_type=jnp.float32)
                * score_scale
            )
            d_keys = (
                d_keys
                + jnp.einsum(
                    "hqk,qhd->khd", d_scores, query_block, preferred_element_type=jnp.float32
                )
                * score_scale
            )
        return (
            jnp.concatenate(d_query_parts, axis=0).reshape(row_count, pair_width),
            d_keys.reshape(key_count, pair_width),
            d_values.reshape(key_count, pair_width),
        )

    d_query_pairs, d_key_pairs, d_value_pairs = lax.map(pair_backward, jnp.arange(pair_count))
    d_query_all = by_rows(d_query_pairs)
    d_keys_all = by_rows(d_key_pairs)
    d_values_all = by_rows(d_value_pairs)
    later_keys, later_values = from_behind(
        (d_keys_all[:row_count], d_values_all[:row_count]), "dev", -1
    )
    front_zeros = jnp.zeros((row_count - row_count, model_width), jnp.float32)
    d_own_keys = d_keys_all[row_count:] + jnp.concatenate([front_zeros, later_keys], axis=0)
    d_own_values = d_values_all[row_count:] + jnp.concatenate([front_zeros, later_values], axis=0)
    _, rotate_pull = jax.vjp(lambda moving: rotate(moving, angles), mixed[:, 0])
    d_query_pre = rotate_pull(d_query_all.reshape(row_count, head_count, HDIM))[0]
    d_key_pre = rotate_pull(d_own_keys.reshape(row_count, head_count, HDIM))[0]
    d_mixed = (
        jnp.stack(
            [d_query_pre, d_key_pre, d_own_values.reshape(row_count, head_count, HDIM)], axis=1
        )
        .reshape(row_count, 3 * model_width)
        .astype(jnp.bfloat16)
    )
    grad_bias_qkv = jnp.sum(d_mixed.astype(jnp.float32), axis=0)
    grad_w_qkv = jnp.einsum("td,te->de", attn_in, d_mixed, preferred_element_type=jnp.float32)
    d_attn_in = jnp.einsum("te,de->td", d_mixed, w_qkv, preferred_element_type=jnp.float32)
    _, norm_pull_a = jax.vjp(
        layer_norm, residual, gain_a.astype(jnp.float32), shift_a.astype(jnp.float32)
    )
    d_attn_tokens, grad_gain_a, grad_shift_a = norm_pull_a(d_attn_in)
    grad_tokens = upstream + d_attn_tokens + d_mlp_tokens
    shards = (
        lax.psum_scatter(grad_gain_a, "dev", scatter_dimension=0, tiled=True),
        lax.psum_scatter(grad_shift_a, "dev", scatter_dimension=0, tiled=True),
        lax.psum_scatter(grad_gain_m, "dev", scatter_dimension=0, tiled=True),
        lax.psum_scatter(grad_shift_m, "dev", scatter_dimension=0, tiled=True),
        lax.psum_scatter(grad_w_qkv, "dev", scatter_dimension=0, tiled=True),
        lax.psum_scatter(grad_bias_qkv, "dev", scatter_dimension=0, tiled=True),
        lax.psum_scatter(grad_w_out, "dev", scatter_dimension=0, tiled=True),
        lax.psum_scatter(grad_bias_out, "dev", scatter_dimension=0, tiled=True),
        lax.psum_scatter(grad_w_up, "dev", scatter_dimension=0, tiled=True),
        lax.psum_scatter(grad_bias_up, "dev", scatter_dimension=0, tiled=True),
        lax.psum_scatter(grad_w_down, "dev", scatter_dimension=0, tiled=True),
        lax.psum_scatter(grad_bias_out, "dev", scatter_dimension=0, tiled=True),
    )
    return (block_out, grad_tokens) + tuple(shards)


def solution(mesh):
    placed = (
        P("dev", None),
        P("dev"),
        P("dev", None),
        P("dev"),
        P("dev"),
        P("dev"),
        P("dev"),
        P("dev", None),
        P("dev"),
        P("dev", None),
        P("dev"),
        P("dev", None),
        P("dev"),
        P("dev", None),
        P("dev"),
    )
    return jax.shard_map(
        local,
        mesh=mesh,
        in_specs=placed,
        out_specs=(
            P("dev", None),
            P("dev", None),
            P("dev"),
            P("dev"),
            P("dev"),
            P("dev"),
            P("dev", None),
            P("dev"),
            P("dev", None),
            P("dev"),
            P("dev", None),
            P("dev"),
            P("dev", None),
            P("dev"),
        ),
        check_vma=False,
    )
```

```python
import functools

import jax
import jax.numpy as jnp
from jax import lax
from jax.experimental import pallas as pl
from jax.experimental.pallas import tpu as pltpu
from jax.sharding import PartitionSpec as P

HDIM = 64
ROT = 16
EPSILON = 1e-05
MASKED = -1e30
BLOCK = 256
VMEM_BYTES = 58 << 20
F32 = jnp.float32
BF16 = jnp.bfloat16
AXIS = "dev"


def params_of(*semantics):
    return pltpu.CompilerParams(dimension_semantics=semantics, vmem_limit_bytes=VMEM_BYTES)


def mm(a, b):
    return lax.dot_general(a, b, (((1,), (0,)), ((), ())), preferred_element_type=F32)


def mm_bt(a, b):
    return lax.dot_general(a, b, (((1,), (1,)), ((), ())), preferred_element_type=F32)


def mm_at(a, b):
    return lax.dot_general(a, b, (((0,), (0,)), ((), ())), preferred_element_type=F32)


def split_axis(count):
    bits = (count // 2).bit_length() - 1
    small = 1 << (bits // 3)
    sizes = [count // 2 // small // small, small, small, 2]
    strides = [small * small * 2, small * 2, 2, 1]
    return sizes, strides


def shifted(value, size, stride, steps):
    count = lax.axis_size(AXIS)
    moves = []
    for source in range(count):
        digit = source // stride % size
        moves.append((source, source + ((digit + steps) % size - digit) * stride))
    return lax.ppermute(value, AXIS, moves)


def place(pieces, digit):
    count = len(pieces)
    if count == 2:
        mine, other = pieces
        first = jnp.where(digit == 0, mine, other)
        second = jnp.where(digit == 0, other, mine)
        return jnp.stack([first, second], axis=1)
    slots = [pieces[0]] * count
    for j in range(count):
        slots[j] = lax.select_n((digit - j) % count, *pieces)
    return jnp.stack(slots, axis=1)


def gather(value, order):
    sizes, strides = split_axis(lax.axis_size(AXIS))
    rows, width = value.shape
    held = [1, 1, 1, 1]
    me = lax.axis_index(AXIS)
    for dim in order:
        size = sizes[dim]
        digit = me // strides[dim] % size
        outer = 1
        inner = rows
        for d in range(4):
            if d < dim:
                outer *= held[d]
            if d > dim:
                inner *= held[d]
        piece = value.reshape(outer, inner, width)
        pieces = [piece] + [shifted(piece, size, strides[dim], s) for s in range(1, size)]
        value = place(pieces, digit)
        held[dim] = size
    return value.reshape(lax.axis_size(AXIS) * rows, width)


def scatter(value, order):
    sizes, strides = split_axis(lax.axis_size(AXIS))
    width = value.shape[1]
    rows = value.shape[0] // lax.axis_size(AXIS)
    held = list(sizes)
    me = lax.axis_index(AXIS)
    kind = value.dtype
    for dim in order:
        size = sizes[dim]
        digit = me // strides[dim] % size
        outer = 1
        inner = rows
        for d in range(4):
            if d < dim:
                outer *= held[d]
            if d > dim:
                inner *= held[d]
        parts = value.reshape(outer, size, inner, width)

        def part(at):
            return lax.dynamic_index_in_dim(parts, at, 1, keepdims=False)

        total = part(digit).astype(F32)
        for s in range(1, size):
            total = total + shifted(part((digit + s) % size), size, strides[dim], s).astype(F32)
        held[dim] = 1
        value = total if dim == order[-1] else total.astype(kind)
    return value.reshape(rows, width)


def from_behind(value, steps):
    count = lax.axis_size(AXIS)
    leading, last = (max(0, -steps), min(count, count - steps))
    return lax.ppermute(value, AXIS, [(source, source + steps) for source in range(leading, last)])


def normalize(values):
    center = values - jnp.mean(values, axis=-1, keepdims=True)
    spread = jnp.mean(center * center, axis=-1, keepdims=True)
    scale = lax.rsqrt(spread + EPSILON)
    return center * scale, scale


def norm_back(tokens, error, gain):
    normal, scale = normalize(tokens)
    scaled = error * gain
    first = jnp.mean(scaled, axis=-1, keepdims=True)
    second = jnp.mean(scaled * normal, axis=-1, keepdims=True)
    return scale * (scaled - first - normal * second), error * normal


def turn(values, table, sign):
    cosine = table[0]
    back = pltpu.roll(values, 120, 1) * table[1]
    ahead = pltpu.roll(values, 8, 1) * table[2]
    return values * cosine + sign * (back + ahead)


def qkv_body(x_ref, gain_ref, shift_ref, w_ref, b_ref, table_ref, out_ref, in_ref):
    width = x_ref.shape[1]
    normal, _ = normalize(x_ref[...].astype(F32))
    rows_in = (normal * gain_ref[...] + shift_ref[...]).astype(BF16)
    in_ref[...] = rows_in
    for j in range(0, out_ref.shape[1], 256):
        mixed = mm(rows_in, w_ref[:, j : j + 256]) + b_ref[:, j : j + 256]
        if j < 2 * width:
            for c in (0, 128):
                out_ref[:, j + c : j + c + 128] = turn(
                    mixed[:, c : c + 128], table_ref, 1.0
                ).astype(BF16)
        else:
            out_ref[:, j : j + 256] = mixed.astype(BF16)


def project(tokens, gain, shift, weight, bias, table):
    rows, width = tokens.shape
    total = 3 * width
    whole = lambda i: (0, 0)
    return pl.pallas_call(
        qkv_body,
        grid=(rows // BLOCK,),
        in_specs=[
            pl.BlockSpec((BLOCK, width), lambda i: (i, 0)),
            pl.BlockSpec((1, width), whole),
            pl.BlockSpec((1, width), whole),
            pl.BlockSpec(weight.shape, whole),
            pl.BlockSpec((1, total), whole),
            pl.BlockSpec((3, BLOCK, 128), lambda i: (0, i, 0)),
        ],
        out_specs=[
            pl.BlockSpec((BLOCK, total), lambda i: (i, 0)),
            pl.BlockSpec((BLOCK, width), lambda i: (i, 0)),
        ],
        out_shape=[
            jax.ShapeDtypeStruct((rows, total), BF16),
            jax.ShapeDtypeStruct((rows, width), BF16),
        ],
        compiler_params=params_of("arbitrary"),
        cost_estimate=pl.CostEstimate(
            flops=2 * rows * width * total, transcendentals=0, bytes_accessed=16 << 20
        ),
        name="qkv_project",
    )(tokens, gain, shift, weight, bias, table)


def attend_body(
    prior,
    first_ref,
    q_ref,
    k_ref,
    v_ref,
    pk_ref,
    pv_ref,
    dc_ref,
    low_ref,
    table_ref,
    ctx_ref,
    dq_ref,
    dk_ref,
    dv_ref,
    pdk_ref,
    pdv_ref,
    keys,
    vals,
    dk_sum,
    dv_sum,
):
    block = pl.program_id(1)
    lead = prior // BLOCK

    @pl.when(block == 0)
    def _():
        keys[:prior] = pk_ref[...]
        keys[prior:] = k_ref[...]
        vals[:prior] = pv_ref[...]
        vals[prior:] = v_ref[...]
        dk_sum[...] = jnp.zeros_like(dk_sum)
        dv_sum[...] = jnp.zeros_like(dv_sum)

    lane = lax.broadcasted_iota(jnp.int32, (BLOCK, 2 * HDIM), 1)
    heads = (lane < HDIM, lane >= HDIM)
    used = block + lead + 1 - first_ref[block]

    def blocks(count):
        start = (block + lead + 1 - count) * BLOCK
        query = (q_ref[...].astype(F32) * (HDIM**-0.5)).astype(BF16)
        incoming = dc_ref[...]
        low = low_ref[...]
        column = lax.broadcasted_iota(jnp.int32, (BLOCK, BLOCK), 1)
        row = lax.broadcasted_iota(jnp.int32, (BLOCK, BLOCK), 0)
        spans = [pl.ds(pl.multiple_of(start + b * BLOCK, BLOCK), BLOCK) for b in range(count)]
        ctx, d_query = [], []
        d_keys, d_vals = [[] for _ in spans], [[] for _ in spans]
        for mine in heads:
            own_query = jnp.where(mine, query, jnp.zeros_like(query))
            own_incoming = jnp.where(mine, incoming, jnp.zeros_like(incoming))
            scores = []
            for b, span in enumerate(spans):
                score = mm_bt(own_query, keys[span])
                allowed = column >= low - (start + b * BLOCK)
                if b == count - 1:
                    allowed = allowed & (column <= row)
                scores.append(jnp.where(allowed, score, MASKED))
            highest = functools.reduce(jnp.maximum, scores)
            highest = jnp.max(highest, axis=-1, keepdims=True)
            grown = [jnp.exp(score - highest) for score in scores]
            normal = jnp.sum(functools.reduce(jnp.add, grown), axis=-1, keepdims=True)
            inverse = 1.0 / normal
            probs = [g * inverse for g in grown]
            low_probs = [p.astype(BF16) for p in probs]
            d_probs = [mm_bt(own_incoming, vals[span]) for span in spans]
            inner = functools.reduce(jnp.add, [p * d for p, d in zip(probs, d_probs)])
            inner = jnp.sum(inner, axis=-1, keepdims=True)
            d_scores = [(p * (d - inner)).astype(BF16) for p, d in zip(probs, d_probs)]
            ctx.append(functools.reduce(jnp.add, [mm(p, vals[s]) for p, s in zip(low_probs, spans)]))
            d_query.append(
                functools.reduce(jnp.add, [mm(d, keys[s]) for d, s in zip(d_scores, spans)])
            )
            for b in range(count):
                d_keys[b].append(mm_at(d_scores[b], query))
                d_vals[b].append(mm_at(low_probs[b], incoming))
        ctx_ref[...] = jnp.where(heads[0], ctx[0], ctx[1]).astype(BF16)
        both = jnp.where(heads[0], d_query[0], d_query[1]) * (HDIM**-0.5)
        dq_ref[...] = turn(both, table_ref, -1.0).astype(BF16)
        for b, span in enumerate(spans):
            dk_sum[span] += jnp.where(heads[0], d_keys[b][0], d_keys[b][1])
            dv_sum[span] += jnp.where(heads[0], d_vals[b][0], d_vals[b][1])

    most = k_ref.shape[0] // BLOCK + 1
    for count in range(1, most + 1):
        pl.when(used == count)(functools.partial(blocks, count))

    @pl.when(block == pl.num_programs(1) - 1)
    def _():
        pdk_ref[...] = dk_sum[:prior].astype(BF16)
        pdv_ref[...] = dv_sum[:prior].astype(BF16)
        dk_ref[...] = dk_sum[prior:]
        dv_ref[...] = dv_sum[prior:]


def attend(first, qkv, before, d_context, low, table):
    rows, width = d_context.shape
    prior = before.shape[0]
    pairs = width // 128
    wide = lambda off: (lambda p, i, f: (0, off + p))
    tile = lambda p, i, f: (i, p)
    return pl.pallas_call(
        functools.partial(attend_body, prior),
        grid_spec=pltpu.PrefetchScalarGridSpec(
            num_scalar_prefetch=1,
            grid=(pairs, rows // BLOCK),
            in_specs=[
                pl.BlockSpec((BLOCK, 128), tile),
                pl.BlockSpec((rows, 128), wide(pairs)),
                pl.BlockSpec((rows, 128), wide(2 * pairs)),
                pl.BlockSpec((prior, 128), wide(0)),
                pl.BlockSpec((prior, 128), wide(pairs)),
                pl.BlockSpec((BLOCK, 128), tile),
                pl.BlockSpec((BLOCK, 1), lambda p, i, f: (i, 0)),
                pl.BlockSpec((3, BLOCK, 128), lambda p, i, f: (0, i, 0)),
            ],
            out_specs=[
                pl.BlockSpec((BLOCK, 128), tile),
                pl.BlockSpec((BLOCK, 128), tile),
                pl.BlockSpec((rows, 128), wide(0)),
                pl.BlockSpec((rows, 128), wide(0)),
                pl.BlockSpec((prior, 128), wide(0)),
                pl.BlockSpec((prior, 128), wide(0)),
            ],
            scratch_shapes=[
                pltpu.VMEM((prior + rows, 128), BF16),
                pltpu.VMEM((prior + rows, 128), BF16),
                pltpu.VMEM((prior + rows, 128), F32),
                pltpu.VMEM((prior + rows, 128), F32),
            ],
        ),
        out_shape=[
            jax.ShapeDtypeStruct((rows, width), BF16),
            jax.ShapeDtypeStruct((rows, width), BF16),
            jax.ShapeDtypeStruct((rows, width), F32),
            jax.ShapeDtypeStruct((rows, width), F32),
            jax.ShapeDtypeStruct((prior, width), BF16),
            jax.ShapeDtypeStruct((prior, width), BF16),
        ],
        compiler_params=params_of("arbitrary", "arbitrary"),
        cost_estimate=pl.CostEstimate(
            flops=50 * 10**9, transcendentals=10**7, bytes_accessed=24 << 20
        ),
        name="attend",
    )(first, qkv, qkv, qkv, before, before, d_context, low, table)


def mlp_body(
    x_ref,
    cot_ref,
    gain_ref,
    shift_ref,
    up_ref,
    bias_ref,
    down_ref,
    ffn_ref,
    d_up_ref,
    d_down_ref,
    d_bias_ref,
    back_ref,
    d_gain_ref,
    d_shift_ref,
    d_out_ref,
    in_ref,
    active,
    d_hidden,
):
    step = pl.program_id(0)
    rows = x_ref.shape[0]
    spans = [slice(r, r + BLOCK) for r in range(0, rows, BLOCK)]

    @pl.when(step == 0)
    def _():
        for s in spans:
            normal, _ = normalize(x_ref[s].astype(F32))
            in_ref[s] = (normal * gain_ref[...] + shift_ref[...]).astype(BF16)
        ffn_ref[...] = jnp.zeros_like(ffn_ref)
        back_ref[...] = jnp.zeros_like(back_ref)
        d_out_ref[...] = jnp.sum(cot_ref[...].astype(F32), axis=0, keepdims=True)

    summed = 0.0
    for s in spans:
        hidden = mm(in_ref[s], up_ref[...]) + bias_ref[...]
        d_active = mm_bt(cot_ref[s], down_ref[...])
        phi = 0.5 + 0.5 * lax.erf(hidden * (0.5**0.5))
        density = jnp.exp(hidden * hidden * -0.5) * 0.3989422804014327
        active[s] = (hidden * phi).astype(BF16)
        moved = (d_active * (phi + hidden * density)).astype(BF16)
        d_hidden[s] = moved
        summed = summed + jnp.sum(moved.astype(F32), axis=0, keepdims=True)
    d_bias_ref[...] = summed
    d_down_ref[...] = mm_at(active[...], cot_ref[...]).astype(BF16)
    d_up_ref[...] = mm_at(in_ref[...], d_hidden[...]).astype(BF16)
    for s in spans:
        ffn_ref[s] += mm(active[s], down_ref[...])
        back_ref[s] += mm_bt(d_hidden[s], up_ref[...])

    @pl.when(step == pl.num_programs(0) - 1)
    def _():
        d_gain, d_shift = 0.0, 0.0
        for s in spans:
            error = back_ref[s]
            moved, product = norm_back(x_ref[s].astype(F32), error, gain_ref[...])
            d_gain = d_gain + jnp.sum(product, axis=0, keepdims=True)
            d_shift = d_shift + jnp.sum(error, axis=0, keepdims=True)
            back_ref[s] = cot_ref[s].astype(F32) + moved
        d_gain_ref[...] = d_gain
        d_shift_ref[...] = d_shift


def mlp(tokens, cotangent, gain, shift, up, up_bias, down):
    rows, width = tokens.shape
    ff = down.shape[0]
    tile = 512
    whole = lambda j: (0, 0)
    vector = pl.BlockSpec((1, width), whole)
    full = pl.BlockSpec((rows, width), whole)
    return pl.pallas_call(
        mlp_body,
        grid=(ff // tile,),
        in_specs=[
            full,
            full,
            vector,
            vector,
            pl.BlockSpec((width, tile), lambda j: (0, j)),
            pl.BlockSpec((1, tile), lambda j: (0, j)),
            pl.BlockSpec((tile, width), lambda j: (j, 0)),
        ],
        out_specs=[
            full,
            pl.BlockSpec((width, tile), lambda j: (0, j)),
            pl.BlockSpec((tile, width), lambda j: (j, 0)),
            pl.BlockSpec((1, tile), lambda j: (0, j)),
            full,
            vector,
            vector,
            vector,
        ],
        out_shape=[
            jax.ShapeDtypeStruct((rows, width), F32),
            jax.ShapeDtypeStruct((width, ff), BF16),
            jax.ShapeDtypeStruct((ff, width), BF16),
            jax.ShapeDtypeStruct((1, ff), F32),
            jax.ShapeDtypeStruct((rows, width), F32),
            jax.ShapeDtypeStruct((1, width), F32),
            jax.ShapeDtypeStruct((1, width), F32),
            jax.ShapeDtypeStruct((1, width), F32),
        ],
        scratch_shapes=[
            pltpu.VMEM((rows, width), BF16),
            pltpu.VMEM((rows, tile), BF16),
            pltpu.VMEM((rows, tile), BF16),
        ],
        compiler_params=params_of("arbitrary"),
        cost_estimate=pl.CostEstimate(
            flops=12 * rows * width * ff, transcendentals=2 * rows * ff, bytes_accessed=30 << 20
        ),
        name="mlp",
    )(tokens, cotangent, gain, shift, up, up_bias, down)


def back_body(
    per_part,
    x_ref,
    in_ref,
    gain_ref,
    w_ref,
    dq_ref,
    dk_ref,
    dv_ref,
    hk_ref,
    hv_ref,
    table_ref,
    rest_ref,
    d_w_ref,
    d_bias_ref,
    grad_ref,
    d_gain_ref,
    d_shift_ref,
    moved,
):
    step = pl.program_id(0)
    rows = x_ref.shape[0]
    own = rows - hk_ref.shape[0]
    spans = [slice(r, r + BLOCK) for r in range(0, rows, BLOCK)]

    @pl.when(step == 0)
    def _():
        grad_ref[...] = jnp.zeros_like(grad_ref)

    @pl.when(step < per_part)
    def _():
        moved[...] = dq_ref[...]

    @pl.when((step >= per_part) & (step < 2 * per_part))
    def _():
        for s in spans:
            for c in range(0, moved.shape[1], 128):
                part = dk_ref[s, c : c + 128]
                if s.start >= own:
                    part = part + hk_ref[s.start - own : s.stop - own, c : c + 128].astype(F32)
                moved[s, c : c + 128] = turn(part, table_ref[:, s], -1.0).astype(BF16)

    @pl.when(step >= 2 * per_part)
    def _():
        for s in spans:
            part = dv_ref[s]
            if s.start >= own:
                part = part + hv_ref[s.start - own : s.stop - own].astype(F32)
            moved[s] = part.astype(BF16)

    d_bias_ref[...] = jnp.sum(moved[...].astype(F32), axis=0, keepdims=True)
    d_w_ref[...] = mm_at(in_ref[...], moved[...]).astype(BF16)
    for s in spans:
        grad_ref[s] += mm_bt(moved[s], w_ref[...])

    @pl.when(step == pl.num_programs(0) - 1)
    def _():
        d_gain, d_shift = 0.0, 0.0
        for s in spans:
            error = grad_ref[s]
            back, product = norm_back(x_ref[s].astype(F32), error, gain_ref[...])
            d_gain = d_gain + jnp.sum(product, axis=0, keepdims=True)
            d_shift = d_shift + jnp.sum(error, axis=0, keepdims=True)
            grad_ref[s] = rest_ref[s] + back
        d_gain_ref[...] = d_gain
        d_shift_ref[...] = d_shift


def back(tokens, attn_in, gain, weight, dq, dk, dv, halo_k, halo_v, table, rest):
    rows, width = tokens.shape
    tile = 256
    per = width // tile
    total = 3 * width
    prior = halo_k.shape[0]
    whole = lambda j: (0, 0)
    vector = pl.BlockSpec((1, width), whole)
    full = pl.BlockSpec((rows, width), whole)
    near = lambda off: (lambda j: (0, jnp.clip(j - off, 0, per - 1)))
    return pl.pallas_call(
        functools.partial(back_body, per),
        grid=(total // tile,),
        in_specs=[
            full,
            full,
            vector,
            pl.BlockSpec((width, tile), lambda j: (0, j)),
            pl.BlockSpec((rows, tile), near(0)),
            pl.BlockSpec((rows, tile), near(per)),
            pl.BlockSpec((rows, tile), near(2 * per)),
            pl.BlockSpec((prior, tile), near(per)),
            pl.BlockSpec((prior, tile), near(2 * per)),
            pl.BlockSpec((3, rows, 128), lambda j: (0, 0, 0)),
            full,
        ],
        out_specs=[
            pl.BlockSpec((width, tile), lambda j: (0, j)),
            pl.BlockSpec((1, tile), lambda j: (0, j)),
            full,
            vector,
            vector,
        ],
        out_shape=[
            jax.ShapeDtypeStruct((width, total), BF16),
            jax.ShapeDtypeStruct((1, total), F32),
            jax.ShapeDtypeStruct((rows, width), F32),
            jax.ShapeDtypeStruct((1, width), F32),
            jax.ShapeDtypeStruct((1, width), F32),
        ],
        scratch_shapes=[pltpu.VMEM((rows, tile), BF16)],
        compiler_params=params_of("arbitrary"),
        cost_estimate=pl.CostEstimate(
            flops=4 * rows * width * total, transcendentals=0, bytes_accessed=30 << 20
        ),
        name="qkv_back",
    )(tokens, attn_in, gain, weight, dq, dk, dv, halo_k, halo_v, table, rest)


def local(
    tokens,
    seq_ids,
    cotangent,
    attn_gain,
    attn_shift,
    mlp_gain,
    mlp_shift,
    qkv_weight,
    qkv_bias,
    out_weight,
    out_bias,
    up_weight,
    up_bias,
    down_weight,
    down_bias,
):
    rows, width = tokens.shape
    own = attn_gain.shape[0]
    prior = rows // 2
    vectors = (
        attn_gain,
        attn_shift,
        mlp_gain,
        mlp_shift,
        qkv_bias,
        out_bias,
        up_bias,
        down_bias,
    )
    counts = [v.shape[0] // own for v in vectors]
    packed = jnp.concatenate([v.reshape(own, -1) for v in vectors], axis=1)
    packed = jnp.pad(packed, ((0, 0), (0, 128 - packed.shape[1])))

    first_half = gather(jnp.concatenate([qkv_weight, packed], axis=1), (0, 2, 1, 3))
    w_down = gather(down_weight, (0, 1, 2, 3))
    second = gather(jnp.concatenate([up_weight, out_weight], axis=1), (1, 2, 0, 3))
    w_out = second[:, up_weight.shape[1] :]
    flat, at = [], qkv_weight.shape[1]
    small = first_half[:, at : at + 128].astype(F32)
    at = 0
    for count in counts:
        flat.append(small[:, at : at + count].reshape(1, -1))
        at += count
    gain_a, shift_a, gain_m, shift_m, b_qkv, b_out, b_up, b_down = flat

    row_index = jnp.arange(rows, dtype=jnp.int32)
    last_id = seq_ids[rows - 1]
    trailing = jnp.sum((seq_ids == last_id).astype(jnp.int32))
    before = from_behind(jnp.stack([last_id, trailing]), 1)
    carry = jnp.where(before[0] == seq_ids[0], before[1], 0)
    smaller = jnp.sum((seq_ids[None, :] < seq_ids[:, None]).astype(jnp.int32), axis=1)
    begins = jnp.where(seq_ids == seq_ids[0], -carry, smaller)
    low = begins + prior
    first_block = low[::BLOCK] // BLOCK
    frequency = 10000.0 ** (-2.0 * jnp.arange(ROT // 2, dtype=F32) / ROT)
    angles = (row_index - begins).astype(F32)[:, None] * frequency[None, :]
    cosine, sine = jnp.cos(angles), jnp.sin(angles)
    lane = jnp.arange(128) % HDIM
    spread = lambda v: jnp.tile(v, (1, 128 // v.shape[1]))
    table = jnp.stack(
        [
            jnp.where(lane < ROT, spread(cosine), 1.0),
            jnp.where(lane < ROT // 2, -spread(sine), 0.0),
            jnp.where((lane >= ROT // 2) & (lane < ROT), spread(sine), 0.0),
        ]
    )

    qkv, attn_in = project(tokens, gain_a, shift_a, first_half, b_qkv, table)
    halo = from_behind(qkv[rows - prior :, width:], 1)
    ffn, d_up, d_down, d_up_bias, rest, d_gain_m, d_shift_m, d_out_bias = mlp(
        tokens, cotangent, gain_m, shift_m, second, b_up, w_down
    )
    d_context = mm_bt(cotangent, w_out).astype(BF16)
    context, dq, dk, dv, back_k, back_v = attend(
        first_block, qkv, halo, d_context, low[:, None], table
    )
    halo_k = from_behind(back_k, -1)
    halo_v = from_behind(back_v, -1)
    block_out = (tokens.astype(F32) + (mm(context, w_out) + b_out) + (ffn + b_down)).astype(BF16)
    d_out = mm_at(context, cotangent).astype(BF16)
    d_qkv, d_qkv_bias, grad_tokens, d_gain_a, d_shift_a = back(
        tokens, attn_in, gain_a, first_half, dq, dk, dv, halo_k, halo_v, table, rest
    )

    d_down = scatter(d_down, (3, 2, 1, 0))
    d_up = scatter(d_up, (3, 0, 2, 1))
    d_out = scatter(d_out, (3, 1, 0, 2))
    d_qkv = scatter(d_qkv, (3, 1, 0, 2))
    sums = (
        d_gain_a,
        d_shift_a,
        d_gain_m,
        d_shift_m,
        d_qkv_bias,
        d_out_bias,
        d_up_bias,
    )
    wide = jnp.concatenate([s.reshape(width, -1) for s in sums], axis=1)
    wide = jnp.pad(wide, ((0, 0), (0, 128 - wide.shape[1])))
    wide = scatter(wide, (3, 2, 1, 0))
    out, at = [], 0
    for s in sums:
        count = s.shape[1] // width
        out.append(wide[:, at : at + count].reshape(-1))
        at += count
    g_gain_a, g_shift_a, g_gain_m, g_shift_m, g_qkv_b, g_out_b, g_up_b = out
    return (
        block_out,
        grad_tokens,
        g_gain_a,
        g_shift_a,
        g_gain_m,
        g_shift_m,
        d_qkv,
        g_qkv_b,
        d_out,
        g_out_b,
        d_up,
        g_up_b,
        d_down,
        g_out_b,
    )


def solution(mesh):
    wide, thin = P("dev", None), P("dev")
    return jax.shard_map(
        local,
        mesh=mesh,
        in_specs=(
            wide,
            thin,
            wide,
            thin,
            thin,
            thin,
            thin,
            wide,
            thin,
            wide,
            thin,
            wide,
            thin,
            wide,
            thin,
        ),
        out_specs=(
            wide,
            wide,
            thin,
            thin,
            thin,
            thin,
            wide,
            thin,
            wide,
            thin,
            wide,
            thin,
            wide,
            thin,
        ),
        check_vma=False,
    )
```

```python
import functools

import jax
import jax.numpy as jnp
from jax import lax
from jax.experimental import pallas as pl
from jax.experimental.pallas import tpu as pltpu
from jax.sharding import PartitionSpec as P

HDIM = 64
ROT = 16
EPSILON = 1e-05
MASKED = -1e30
BLOCK = 256
VMEM_BYTES = 58 << 20
F32 = jnp.float32
BF16 = jnp.bfloat16
AXIS = "dev"


def params_of(*semantics):
    return pltpu.CompilerParams(dimension_semantics=semantics, vmem_limit_bytes=VMEM_BYTES)


def mm(a, b):
    return lax.dot_general(a, b, (((1,), (0,)), ((), ())), preferred_element_type=F32)


def mm_bt(a, b):
    return lax.dot_general(a, b, (((1,), (1,)), ((), ())), preferred_element_type=F32)


def mm_at(a, b):
    return lax.dot_general(a, b, (((0,), (0,)), ((), ())), preferred_element_type=F32)


def split_axis(count):
    bits = (count // 2).bit_length() - 1
    small = 1 << (bits // 3)
    sizes = [count // 2 // small // small, small, small, 2]
    strides = [small * small * 2, small * 2, 2, 1]
    return sizes, strides


def shifted(value, size, stride, steps):
    count = lax.axis_size(AXIS)
    moves = []
    for source in range(count):
        digit = source // stride % size
        moves.append((source, source + ((digit + steps) % size - digit) * stride))
    return lax.ppermute(value, AXIS, moves)


def place(pieces, digit):
    count = len(pieces)
    if count == 2:
        mine, other = pieces
        first = jnp.where(digit == 0, mine, other)
        second = jnp.where(digit == 0, other, mine)
        return jnp.stack([first, second], axis=1)
    slots = [pieces[0]] * count
    for j in range(count):
        slots[j] = lax.select_n((digit - j) % count, *pieces)
    return jnp.stack(slots, axis=1)


class Gather:
    def __init__(self, value, order):
        self.sizes, self.strides = split_axis(lax.axis_size(AXIS))
        self.value, self.order = value, list(order)
        self.rows, self.width = value.shape
        self.held = [1, 1, 1, 1]

    def step(self):
        dim = self.order.pop(0)
        size, stride = self.sizes[dim], self.strides[dim]
        digit = lax.axis_index(AXIS) // stride % size
        outer, inner = 1, self.rows
        for d in range(4):
            if d < dim:
                outer *= self.held[d]
            if d > dim:
                inner *= self.held[d]
        piece = self.value.reshape(outer, inner, self.width)
        pieces = [piece] + [shifted(piece, size, stride, s) for s in range(1, size)]
        self.value = place(pieces, digit)
        self.held[dim] = size

    def whole(self):
        return self.value.reshape(lax.axis_size(AXIS) * self.rows, self.width)


class Scatter:
    def __init__(self, value, order):
        self.sizes, self.strides = split_axis(lax.axis_size(AXIS))
        self.value, self.order, self.kind = value, list(order), value.dtype
        self.rows = value.shape[0] // lax.axis_size(AXIS)
        self.held = list(self.sizes)

    def step(self):
        dim = self.order.pop(0)
        size, stride = self.sizes[dim], self.strides[dim]
        digit = lax.axis_index(AXIS) // stride % size
        outer, inner = 1, self.rows
        for d in range(4):
            if d < dim:
                outer *= self.held[d]
            if d > dim:
                inner *= self.held[d]
        parts = self.value.reshape(outer, size, inner, self.value.shape[-1])

        def part(at):
            return lax.dynamic_index_in_dim(parts, at, 1, keepdims=False)

        total = part(digit).astype(F32)
        for s in range(1, size):
            total = total + shifted(part((digit + s) % size), size, stride, s).astype(F32)
        self.held[dim] = 1
        self.value = total.astype(self.kind) if self.order else total
        return self.value

    def rest(self):
        while self.order:
            self.step()
        return self.value.reshape(self.rows, -1)


def together(*chains):
    values = lax.optimization_barrier(tuple(c.value for c in chains))
    for chain, value in zip(chains, values):
        chain.value = value


def behind(value, *chains):
    values = lax.optimization_barrier((value, *[c.value for c in chains]))
    for chain, held in zip(chains, values[1:]):
        chain.value = held


def from_behind(value, steps):
    count = lax.axis_size(AXIS)
    leading, last = (max(0, -steps), min(count, count - steps))
    return lax.ppermute(value, AXIS, [(source, source + steps) for source in range(leading, last)])


def normalize(values):
    center = values - jnp.mean(values, axis=-1, keepdims=True)
    spread = jnp.mean(center * center, axis=-1, keepdims=True)
    scale = lax.rsqrt(spread + EPSILON)
    return center * scale, scale


def norm_back(tokens, error, gain):
    normal, scale = normalize(tokens)
    scaled = error * gain
    first = jnp.mean(scaled, axis=-1, keepdims=True)
    second = jnp.mean(scaled * normal, axis=-1, keepdims=True)
    return scale * (scaled - first - normal * second), error * normal


def turn(values, table, sign):
    cosine = table[0]
    back = pltpu.roll(values, 120, 1) * table[1]
    ahead = pltpu.roll(values, 8, 1) * table[2]
    return values * cosine + sign * (back + ahead)


def qkv_body(cut, x_ref, gain_ref, shift_ref, w_ref, v_ref, b_ref, table_ref, out_ref, in_ref):
    width = x_ref.shape[1]
    normal, _ = normalize(x_ref[...].astype(F32))
    rows_in = (normal * gain_ref[...] + shift_ref[...]).astype(BF16)
    in_ref[...] = rows_in
    for j in range(0, out_ref.shape[1], 256):
        tile = w_ref[:, j : j + 256] if j < cut else v_ref[:, j - cut : j - cut + 256]
        mixed = mm(rows_in, tile) + b_ref[:, j : j + 256]
        if j < 2 * width:
            for c in (0, 128):
                out_ref[:, j + c : j + c + 128] = turn(
                    mixed[:, c : c + 128], table_ref, 1.0
                ).astype(BF16)
        else:
            out_ref[:, j : j + 256] = mixed.astype(BF16)


def project(tokens, gain, shift, weight, weight_more, bias, table):
    rows, width = tokens.shape
    total = 3 * width
    whole = lambda i: (0, 0)
    return pl.pallas_call(
        functools.partial(qkv_body, weight.shape[1]),
        grid=(rows // BLOCK,),
        in_specs=[
            pl.BlockSpec((BLOCK, width), lambda i: (i, 0)),
            pl.BlockSpec((1, width), whole),
            pl.BlockSpec((1, width), whole),
            pl.BlockSpec(weight.shape, whole),
            pl.BlockSpec(weight_more.shape, whole),
            pl.BlockSpec((1, total), whole),
            pl.BlockSpec((3, BLOCK, 128), lambda i: (0, i, 0)),
        ],
        out_specs=[
            pl.BlockSpec((BLOCK, total), lambda i: (i, 0)),
            pl.BlockSpec((BLOCK, width), lambda i: (i, 0)),
        ],
        out_shape=[
            jax.ShapeDtypeStruct((rows, total), BF16),
            jax.ShapeDtypeStruct((rows, width), BF16),
        ],
        compiler_params=params_of("arbitrary"),
        cost_estimate=pl.CostEstimate(
            flops=2 * rows * width * total, transcendentals=0, bytes_accessed=16 << 20
        ),
        name="qkv_project",
    )(tokens, gain, shift, weight, weight_more, bias, table)


def attend_body(
    prior,
    extra,
    first_ref,
    q_ref,
    k_ref,
    v_ref,
    pk_ref,
    pv_ref,
    dc_ref,
    low_ref,
    table_ref,
    *refs,
):
    ctx_ref, dq_ref, dk_ref, dv_ref, pdk_ref, pdv_ref, keys, vals, dk_sum, dv_sum = refs[extra:]
    block = pl.program_id(1)
    lead = prior // BLOCK

    @pl.when(block == 0)
    def _():
        keys[:prior] = pk_ref[...]
        keys[prior:] = k_ref[...]
        vals[:prior] = pv_ref[...]
        vals[prior:] = v_ref[...]
        dk_sum[...] = jnp.zeros_like(dk_sum)
        dv_sum[...] = jnp.zeros_like(dv_sum)

    lane = lax.broadcasted_iota(jnp.int32, (BLOCK, 2 * HDIM), 1)
    heads = (lane < HDIM, lane >= HDIM)
    used = block + lead + 1 - first_ref[block]

    def blocks(count):
        start = (block + lead + 1 - count) * BLOCK
        query = (q_ref[...].astype(F32) * (HDIM**-0.5)).astype(BF16)
        incoming = dc_ref[...]
        low = low_ref[...]
        column = lax.broadcasted_iota(jnp.int32, (BLOCK, BLOCK), 1)
        row = lax.broadcasted_iota(jnp.int32, (BLOCK, BLOCK), 0)
        spans = [pl.ds(pl.multiple_of(start + b * BLOCK, BLOCK), BLOCK) for b in range(count)]
        ctx, d_query = [], []
        d_keys, d_vals = [[] for _ in spans], [[] for _ in spans]
        for mine in heads:
            own_query = jnp.where(mine, query, jnp.zeros_like(query))
            own_incoming = jnp.where(mine, incoming, jnp.zeros_like(incoming))
            scores = []
            for b, span in enumerate(spans):
                score = mm_bt(own_query, keys[span])
                allowed = column >= low - (start + b * BLOCK)
                if b == count - 1:
                    allowed = allowed & (column <= row)
                scores.append(jnp.where(allowed, score, MASKED))
            highest = functools.reduce(jnp.maximum, scores)
            highest = jnp.max(highest, axis=-1, keepdims=True)
            grown = [jnp.exp(score - highest) for score in scores]
            normal = jnp.sum(functools.reduce(jnp.add, grown), axis=-1, keepdims=True)
            inverse = 1.0 / normal
            probs = [g * inverse for g in grown]
            low_probs = [p.astype(BF16) for p in probs]
            d_probs = [mm_bt(own_incoming, vals[span]) for span in spans]
            inner = functools.reduce(jnp.add, [p * d for p, d in zip(probs, d_probs)])
            inner = jnp.sum(inner, axis=-1, keepdims=True)
            d_scores = [(p * (d - inner)).astype(BF16) for p, d in zip(probs, d_probs)]
            ctx.append(functools.reduce(jnp.add, [mm(p, vals[s]) for p, s in zip(low_probs, spans)]))
            d_query.append(
                functools.reduce(jnp.add, [mm(d, keys[s]) for d, s in zip(d_scores, spans)])
            )
            for b in range(count):
                d_keys[b].append(mm_at(d_scores[b], query))
                d_vals[b].append(mm_at(low_probs[b], incoming))
        ctx_ref[...] = jnp.where(heads[0], ctx[0], ctx[1]).astype(BF16)
        both = jnp.where(heads[0], d_query[0], d_query[1]) * (HDIM**-0.5)
        dq_ref[...] = turn(both, table_ref, -1.0).astype(BF16)
        for b, span in enumerate(spans):
            dk_sum[span] += jnp.where(heads[0], d_keys[b][0], d_keys[b][1])
            dv_sum[span] += jnp.where(heads[0], d_vals[b][0], d_vals[b][1])

    most = k_ref.shape[0] // BLOCK + 1
    for count in range(1, most + 1):
        pl.when(used == count)(functools.partial(blocks, count))

    @pl.when(block == pl.num_programs(1) - 1)
    def _():
        pdk_ref[...] = dk_sum[:prior].astype(BF16)
        pdv_ref[...] = dv_sum[:prior].astype(BF16)
        dk_ref[...] = dk_sum[prior:]
        dv_ref[...] = dv_sum[prior:]


def attend(first, qkv, before, d_context, low, table, begin, count, made=(), after=()):
    rows, width = d_context.shape
    prior = before.shape[0]
    pairs = width // 128
    wide = lambda off: (lambda p, i, f: (0, off + begin + p))
    tile = lambda p, i, f: (i, begin + p)
    extra = (*made, *after)
    return pl.pallas_call(
        functools.partial(attend_body, prior, len(extra)),
        grid_spec=pltpu.PrefetchScalarGridSpec(
            num_scalar_prefetch=1,
            grid=(count, rows // BLOCK),
            in_specs=[
                pl.BlockSpec((BLOCK, 128), tile),
                pl.BlockSpec((rows, 128), wide(pairs)),
                pl.BlockSpec((rows, 128), wide(2 * pairs)),
                pl.BlockSpec((prior, 128), wide(0)),
                pl.BlockSpec((prior, 128), wide(pairs)),
                pl.BlockSpec((BLOCK, 128), tile),
                pl.BlockSpec((BLOCK, 1), lambda p, i, f: (i, 0)),
                pl.BlockSpec((3, BLOCK, 128), lambda p, i, f: (0, i, 0)),
                *[pl.BlockSpec(memory_space=pl.ANY) for _ in extra],
            ],
            out_specs=[
                pl.BlockSpec((BLOCK, 128), tile),
                pl.BlockSpec((BLOCK, 128), tile),
                pl.BlockSpec((rows, 128), wide(0)),
                pl.BlockSpec((rows, 128), wide(0)),
                pl.BlockSpec((prior, 128), lambda p, i, f: (0, p)),
                pl.BlockSpec((prior, 128), lambda p, i, f: (0, p)),
            ],
            scratch_shapes=[
                pltpu.VMEM((prior + rows, 128), BF16),
                pltpu.VMEM((prior + rows, 128), BF16),
                pltpu.VMEM((prior + rows, 128), F32),
                pltpu.VMEM((prior + rows, 128), F32),
            ],
        ),
        out_shape=[
            jax.ShapeDtypeStruct((rows, width), BF16),
            jax.ShapeDtypeStruct((rows, width), BF16),
            jax.ShapeDtypeStruct((rows, width), F32),
            jax.ShapeDtypeStruct((rows, width), F32),
            jax.ShapeDtypeStruct((prior, 128 * count), BF16),
            jax.ShapeDtypeStruct((prior, 128 * count), BF16),
        ],
        compiler_params=params_of("arbitrary", "arbitrary"),
        cost_estimate=pl.CostEstimate(
            flops=8 * 10**9 * count, transcendentals=10**6 * count, bytes_accessed=4 * count << 20
        ),
        input_output_aliases={9 + i: i for i in range(len(made))},
        name="attend",
    )(first, qkv, qkv, qkv, before, before, d_context, low, table, *extra)


def mlp_body(
    x_ref,
    cot_ref,
    gain_ref,
    shift_ref,
    up_ref,
    bias_ref,
    down_ref,
    ffn_ref,
    d_up_ref,
    d_down_ref,
    d_bias_ref,
    back_ref,
    d_gain_ref,
    d_shift_ref,
    d_out_ref,
    in_ref,
    active,
    d_hidden,
):
    step = pl.program_id(0)
    rows = x_ref.shape[0]
    spans = [slice(r, r + BLOCK) for r in range(0, rows, BLOCK)]

    @pl.when(step == 0)
    def _():
        for s in spans:
            normal, _ = normalize(x_ref[s].astype(F32))
            in_ref[s] = (normal * gain_ref[...] + shift_ref[...]).astype(BF16)
        ffn_ref[...] = jnp.zeros_like(ffn_ref)
        back_ref[...] = jnp.zeros_like(back_ref)
        d_out_ref[...] = jnp.sum(cot_ref[...].astype(F32), axis=0, keepdims=True)

    summed = 0.0
    for s in spans:
        hidden = mm(in_ref[s], up_ref[...]) + bias_ref[...]
        d_active = mm_bt(cot_ref[s], down_ref[...])
        phi = 0.5 + 0.5 * lax.erf(hidden * (0.5**0.5))
        density = jnp.exp(hidden * hidden * -0.5) * 0.3989422804014327
        active[s] = (hidden * phi).astype(BF16)
        moved = (d_active * (phi + hidden * density)).astype(BF16)
        d_hidden[s] = moved
        summed = summed + jnp.sum(moved.astype(F32), axis=0, keepdims=True)
    d_bias_ref[...] = summed
    d_down_ref[...] = mm_at(active[...], cot_ref[...]).astype(BF16)
    d_up_ref[...] = mm_at(in_ref[...], d_hidden[...]).astype(BF16)
    for s in spans:
        ffn_ref[s] += mm(active[s], down_ref[...])
        back_ref[s] += mm_bt(d_hidden[s], up_ref[...])

    @pl.when(step == pl.num_programs(0) - 1)
    def _():
        d_gain, d_shift = 0.0, 0.0
        for s in spans:
            error = back_ref[s]
            moved, product = norm_back(x_ref[s].astype(F32), error, gain_ref[...])
            d_gain = d_gain + jnp.sum(product, axis=0, keepdims=True)
            d_shift = d_shift + jnp.sum(error, axis=0, keepdims=True)
            back_ref[s] = cot_ref[s].astype(F32) + moved
        d_gain_ref[...] = d_gain
        d_shift_ref[...] = d_shift


def mlp(tokens, cotangent, gain, shift, up, up_bias, down):
    rows, width = tokens.shape
    ff = down.shape[0]
    tile = 512
    whole = lambda j: (0, 0)
    vector = pl.BlockSpec((1, width), whole)
    full = pl.BlockSpec((rows, width), whole)
    return pl.pallas_call(
        mlp_body,
        grid=(ff // tile,),
        in_specs=[
            full,
            full,
            vector,
            vector,
            pl.BlockSpec((width, tile), lambda j: (0, j)),
            pl.BlockSpec((1, tile), lambda j: (0, j)),
            pl.BlockSpec((tile, width), lambda j: (j, 0)),
        ],
        out_specs=[
            full,
            pl.BlockSpec((width, tile), lambda j: (0, j)),
            pl.BlockSpec((tile, width), lambda j: (j, 0)),
            pl.BlockSpec((1, tile), lambda j: (0, j)),
            full,
            vector,
            vector,
            vector,
        ],
        out_shape=[
            jax.ShapeDtypeStruct((rows, width), F32),
            jax.ShapeDtypeStruct((width, ff), BF16),
            jax.ShapeDtypeStruct((ff, width), BF16),
            jax.ShapeDtypeStruct((1, ff), F32),
            jax.ShapeDtypeStruct((rows, width), F32),
            jax.ShapeDtypeStruct((1, width), F32),
            jax.ShapeDtypeStruct((1, width), F32),
            jax.ShapeDtypeStruct((1, width), F32),
        ],
        scratch_shapes=[
            pltpu.VMEM((rows, width), BF16),
            pltpu.VMEM((rows, tile), BF16),
            pltpu.VMEM((rows, tile), BF16),
        ],
        compiler_params=params_of("arbitrary"),
        cost_estimate=pl.CostEstimate(
            flops=12 * rows * width * ff, transcendentals=2 * rows * ff, bytes_accessed=30 << 20
        ),
        name="mlp",
    )(tokens, cotangent, gain, shift, up, up_bias, down)


def back_body(
    per_part,
    x_ref,
    in_ref,
    gain_ref,
    wq_ref,
    wk_ref,
    wv_ref,
    dq_ref,
    dk_ref,
    dv_ref,
    hk_ref,
    hv_ref,
    table_ref,
    rest_ref,
    *refs,
):
    d_wk_ref, d_wv_ref, d_bias_ref, grad_ref, d_gain_ref, d_shift_ref, moved = refs[-7:]
    step = pl.program_id(0)
    rows = x_ref.shape[0]
    own = rows - hk_ref.shape[0]
    spans = [slice(r, r + BLOCK) for r in range(0, rows, BLOCK)]

    @pl.when(step == 0)
    def _():
        for s in spans:
            grad_ref[s] = mm_bt(dq_ref[s], wq_ref[...])

    @pl.when(step < per_part)
    def _():
        for s in spans:
            for c in range(0, moved.shape[1], 128):
                part = dk_ref[s, c : c + 128]
                if s.start >= own:
                    part = part + hk_ref[s.start - own : s.stop - own, c : c + 128].astype(F32)
                moved[s, c : c + 128] = turn(part, table_ref[:, s], -1.0).astype(BF16)
        d_wk_ref[...] = mm_at(in_ref[...], moved[...]).astype(BF16)
        for s in spans:
            grad_ref[s] += mm_bt(moved[s], wk_ref[...])

    @pl.when(step >= per_part)
    def _():
        for s in spans:
            part = dv_ref[s]
            if s.start >= own:
                part = part + hv_ref[s.start - own : s.stop - own].astype(F32)
            moved[s] = part.astype(BF16)
        d_wv_ref[...] = mm_at(in_ref[...], moved[...]).astype(BF16)
        for s in spans:
            grad_ref[s] += mm_bt(moved[s], wv_ref[...])

    d_bias_ref[...] = jnp.sum(moved[...].astype(F32), axis=0, keepdims=True)

    @pl.when(step == pl.num_programs(0) - 1)
    def _():
        d_gain, d_shift = 0.0, 0.0
        for s in spans:
            error = grad_ref[s]
            back, product = norm_back(x_ref[s].astype(F32), error, gain_ref[...])
            d_gain = d_gain + jnp.sum(product, axis=0, keepdims=True)
            d_shift = d_shift + jnp.sum(error, axis=0, keepdims=True)
            grad_ref[s] = rest_ref[s] + back
        d_gain_ref[...] = d_gain
        d_shift_ref[...] = d_shift


def back(tokens, attn_in, gain, weight, weight_more, dq, dk, dv, halo_k, halo_v, table, rest, after):
    rows, width = tokens.shape
    tile = 256
    per = width // tile
    prior = halo_k.shape[0]
    whole = lambda j: (0, 0)
    vector = pl.BlockSpec((1, width), whole)
    full = pl.BlockSpec((rows, width), whole)
    near = lambda off: (lambda j: (0, jnp.clip(j - off, 0, per - 1)))
    return pl.pallas_call(
        functools.partial(back_body, per),
        grid=(2 * per,),
        in_specs=[
            full,
            full,
            vector,
            pl.BlockSpec((width, width), whole),
            pl.BlockSpec((width, tile), lambda j: (0, per + jnp.clip(j, 0, per - 1))),
            pl.BlockSpec((width, tile), near(per)),
            full,
            pl.BlockSpec((rows, tile), near(0)),
            pl.BlockSpec((rows, tile), near(per)),
            pl.BlockSpec((prior, tile), near(0)),
            pl.BlockSpec((prior, tile), near(per)),
            pl.BlockSpec((3, rows, 128), lambda j: (0, 0, 0)),
            full,
            *[pl.BlockSpec(memory_space=pl.ANY) for _ in after],
        ],
        out_specs=[
            pl.BlockSpec((width, tile), near(0)),
            pl.BlockSpec((width, tile), near(per)),
            pl.BlockSpec((1, tile), lambda j: (0, j)),
            full,
            vector,
            vector,
        ],
        out_shape=[
            jax.ShapeDtypeStruct((width, width), BF16),
            jax.ShapeDtypeStruct((width, width), BF16),
            jax.ShapeDtypeStruct((1, 2 * width), F32),
            jax.ShapeDtypeStruct((rows, width), F32),
            jax.ShapeDtypeStruct((1, width), F32),
            jax.ShapeDtypeStruct((1, width), F32),
        ],
        scratch_shapes=[pltpu.VMEM((rows, tile), BF16)],
        compiler_params=params_of("arbitrary"),
        cost_estimate=pl.CostEstimate(
            flops=10 * rows * width * width, transcendentals=0, bytes_accessed=30 << 20
        ),
        name="qkv_back",
    )(tokens, attn_in, gain, weight, weight, weight_more, dq, dk, dv, halo_k, halo_v, table, rest, *after)


def local(
    tokens,
    seq_ids,
    cotangent,
    attn_gain,
    attn_shift,
    mlp_gain,
    mlp_shift,
    qkv_weight,
    qkv_bias,
    out_weight,
    out_bias,
    up_weight,
    up_bias,
    down_weight,
    down_bias,
):
    rows, width = tokens.shape
    own = attn_gain.shape[0]
    prior = rows // 2
    vectors = (
        attn_gain,
        attn_shift,
        mlp_gain,
        mlp_shift,
        qkv_bias,
        out_bias,
        up_bias,
        down_bias,
    )
    count = lax.axis_size(AXIS)
    packed = jnp.concatenate(vectors)
    packed = jnp.pad(packed, (0, own * 128 - packed.shape[0])).reshape(own, 128)

    w_first = Gather(qkv_weight[:, : 2 * width], (0, 1, 2, 3))
    w_then = Gather(
        jnp.concatenate([qkv_weight[:, 2 * width :], out_weight, packed], axis=1), (0, 2, 1, 3)
    )
    w_up, w_down = Gather(up_weight, (0, 2, 1, 3)), Gather(down_weight, (0, 1, 2, 3))
    w_first.step(), w_then.step()
    behind(w_first.value, w_up, w_down, w_then)
    for _ in range(3):
        together(w_first, w_then)
        w_first.step(), w_then.step()
    w_up.step(), w_down.step()
    for _ in range(3):
        together(w_up, w_down)
        w_up.step(), w_down.step()
    w_first, w_then, w_up, w_down = [w.whole() for w in (w_first, w_then, w_up, w_down)]
    w_out = w_then[:, width : 2 * width]
    small = w_then[:, 2 * width :].reshape(count, own * 128).astype(F32)
    flat, at = [], 0
    for v in vectors:
        flat.append(small[:, at : at + v.shape[0]].reshape(1, -1))
        at += v.shape[0]
    gain_a, shift_a, gain_m, shift_m, b_qkv, b_out, b_up, b_down = flat

    row_index = jnp.arange(rows, dtype=jnp.int32)
    last_id = seq_ids[rows - 1]
    trailing = jnp.sum((seq_ids == last_id).astype(jnp.int32))
    before = from_behind(jnp.stack([last_id, trailing]), 1)
    carry = jnp.where(before[0] == seq_ids[0], before[1], 0)
    smaller = jnp.sum((seq_ids[None, :] < seq_ids[:, None]).astype(jnp.int32), axis=1)
    begins = jnp.where(seq_ids == seq_ids[0], -carry, smaller)
    low = begins + prior
    first_block = low[::BLOCK] // BLOCK
    frequency = 10000.0 ** (-2.0 * jnp.arange(ROT // 2, dtype=F32) / ROT)
    angles = (row_index - begins).astype(F32)[:, None] * frequency[None, :]
    cosine, sine = jnp.cos(angles), jnp.sin(angles)
    lane = jnp.arange(128) % HDIM
    spread = lambda v: jnp.tile(v, (1, 128 // v.shape[1]))
    table = jnp.stack(
        [
            jnp.where(lane < ROT, spread(cosine), 1.0),
            jnp.where(lane < ROT // 2, -spread(sine), 0.0),
            jnp.where((lane >= ROT // 2) & (lane < ROT), spread(sine), 0.0),
        ]
    )

    qkv, attn_in = project(tokens, gain_a, shift_a, w_first, w_then, b_qkv, table)
    halo = from_behind(qkv[rows - prior :, width:], 1)
    ffn, d_up, d_down, d_up_bias, rest, d_gain_m, d_shift_m, d_out_bias = mlp(
        tokens, cotangent, gain_m, shift_m, w_up, b_up, w_down
    )
    d_up, d_down = Scatter(d_up, (3, 1, 2, 0)), Scatter(d_down, (3, 2, 1, 0))
    d_context = mm_bt(cotangent, w_out).astype(BF16)
    pairs = width // 128
    shared = (first_block, qkv, halo, d_context, low[:, None], table)
    *made, back_k, back_v = attend(*shared, 0, pairs // 2)
    halo_k, halo_v = [from_behind(back_k, -1)], [from_behind(back_v, -1)]
    summed = (d_up.step(), d_down.step())
    *made, back_k, back_v = attend(*shared, pairs // 2, pairs - pairs // 2, made, summed)
    context, dq, dk, dv = made
    halo_k = jnp.concatenate([*halo_k, from_behind(back_k, -1)], axis=1)
    halo_v = jnp.concatenate([*halo_v, from_behind(back_v, -1)], axis=1)
    summed = (d_up.step(), d_down.step())
    (context, dq), _ = lax.optimization_barrier(((context, dq), summed))
    d_out = Scatter(mm_at(context, cotangent).astype(BF16), (3, 1, 2, 0))
    d_wq = Scatter(mm_at(attn_in, dq).astype(BF16), (3, 2, 1, 0))
    d_bias_q = jnp.sum(dq.astype(F32), axis=0, keepdims=True)
    block_out = (tokens.astype(F32) + (mm(context, w_out) + b_out) + (ffn + b_down)).astype(BF16)
    summed = (d_out.step(), d_wq.step())
    d_wk, d_wv, d_bias_kv, grad_tokens, d_gain_a, d_shift_a = back(
        tokens, attn_in, gain_a, w_first, w_then, dq, dk, dv, halo_k, halo_v, table, rest, summed
    )

    d_wk, d_wv = Scatter(d_wk, (3, 1, 2, 0)), Scatter(d_wv, (3, 2, 1, 0))
    d_up.step(), d_down.step()
    together(d_up, d_down, d_out, d_wq, d_wk, d_wv)
    sums = (
        d_gain_a,
        d_shift_a,
        d_gain_m,
        d_shift_m,
        d_bias_q,
        d_bias_kv,
        d_out_bias,
        d_up_bias,
    )
    wide = jnp.concatenate([s[:, :width].reshape(count, -1) for s in sums[:4]], axis=1)
    d_bias = jnp.concatenate([d_bias_q, d_bias_kv], axis=1).reshape(count, -1)
    wide = jnp.concatenate(
        [wide, d_bias, d_out_bias.reshape(count, -1), d_up_bias.reshape(count, -1)], axis=1
    )
    wide = Scatter(wide, (3, 2, 1, 0))
    for at in range(3):
        chains = (d_wk, d_wv, wide, d_out, d_wq)
        for chain in chains:
            chain.step()
        if at < 2:
            together(*chains)
        else:
            together(d_wk, d_wv, wide)
    wide = wide.rest().reshape(-1)
    out, at = [], 0
    for many in (1, 1, 1, 1, 3, 1, 4):
        out.append(wide[at : at + many * own])
        at += many * own
    g_gain_a, g_shift_a, g_gain_m, g_shift_m, g_qkv_b, g_out_b, g_up_b = out
    d_qkv = jnp.concatenate([d_wq.rest(), d_wk.rest(), d_wv.rest()], axis=1)
    d_out, d_up, d_down = d_out.rest(), d_up.rest(), d_down.rest()
    return (
        block_out,
        grad_tokens,
        g_gain_a,
        g_shift_a,
        g_gain_m,
        g_shift_m,
        d_qkv,
        g_qkv_b,
        d_out,
        g_out_b,
        d_up,
        g_up_b,
        d_down,
        g_out_b,
    )


def solution(mesh):
    wide, thin = P("dev", None), P("dev")
    return jax.shard_map(
        local,
        mesh=mesh,
        in_specs=(
            wide,
            thin,
            wide,
            thin,
            thin,
            thin,
            thin,
            wide,
            thin,
            wide,
            thin,
            wide,
            thin,
            wide,
            thin,
        ),
        out_specs=(
            wide,
            wide,
            thin,
            thin,
            thin,
            thin,
            wide,
            thin,
            wide,
            thin,
            wide,
            thin,
            wide,
            thin,
        ),
        check_vma=False,
    )
```

```python
import functools

import jax
import jax.numpy as jnp
from jax import lax
from jax.experimental import pallas as pl
from jax.experimental.pallas import tpu as pltpu
from jax.sharding import PartitionSpec as P

HDIM = 64
ROT = 16
EPSILON = 1e-05
MASKED = -1e30
BLOCK = 256
VMEM_BYTES = 58 << 20
F32 = jnp.float32
BF16 = jnp.bfloat16
AXIS = "dev"


def params_of(*semantics):
    return pltpu.CompilerParams(dimension_semantics=semantics, vmem_limit_bytes=VMEM_BYTES)


def mm(a, b):
    return lax.dot_general(a, b, (((1,), (0,)), ((), ())), preferred_element_type=F32)


def mm_bt(a, b):
    return lax.dot_general(a, b, (((1,), (1,)), ((), ())), preferred_element_type=F32)


def mm_at(a, b):
    return lax.dot_general(a, b, (((0,), (0,)), ((), ())), preferred_element_type=F32)


def split_axis(count):
    bits = (count // 2).bit_length() - 1
    small = 1 << (bits // 3)
    sizes = [count // 2 // small // small, small, small, 2]
    strides = [small * small * 2, small * 2, 2, 1]
    return sizes, strides


def shifted(value, size, stride, steps):
    count = lax.axis_size(AXIS)
    moves = []
    for source in range(count):
        digit = source // stride % size
        moves.append((source, source + ((digit + steps) % size - digit) * stride))
    return lax.ppermute(value, AXIS, moves)


def place(pieces, digit):
    count = len(pieces)
    if count == 2:
        mine, other = pieces
        first = jnp.where(digit == 0, mine, other)
        second = jnp.where(digit == 0, other, mine)
        return jnp.stack([first, second], axis=1)
    slots = [pieces[0]] * count
    for j in range(count):
        slots[j] = lax.select_n((digit - j) % count, *pieces)
    return jnp.stack(slots, axis=1)


class Gather:
    def __init__(self, value, order):
        self.sizes, self.strides = split_axis(lax.axis_size(AXIS))
        self.value, self.order = value, list(order)
        self.rows, self.width = value.shape
        self.held = [1, 1, 1, 1]

    def step(self):
        dim = self.order.pop(0)
        size, stride = self.sizes[dim], self.strides[dim]
        digit = lax.axis_index(AXIS) // stride % size
        outer, inner = 1, self.rows
        for d in range(4):
            if d < dim:
                outer *= self.held[d]
            if d > dim:
                inner *= self.held[d]
        piece = self.value.reshape(outer, inner, self.width)
        pieces = [piece] + [shifted(piece, size, stride, s) for s in range(1, size)]
        self.value = place(pieces, digit)
        self.held[dim] = size

    def whole(self):
        return self.value.reshape(lax.axis_size(AXIS) * self.rows, self.width)


class Scatter:
    def __init__(self, value, order):
        self.sizes, self.strides = split_axis(lax.axis_size(AXIS))
        self.value, self.order, self.kind = value, list(order), value.dtype
        self.rows = value.shape[0] // lax.axis_size(AXIS)
        self.held = list(self.sizes)

    def step(self):
        dim = self.order.pop(0)
        size, stride = self.sizes[dim], self.strides[dim]
        digit = lax.axis_index(AXIS) // stride % size
        outer, inner = 1, self.rows
        for d in range(4):
            if d < dim:
                outer *= self.held[d]
            if d > dim:
                inner *= self.held[d]
        parts = self.value.reshape(outer, size, inner, self.value.shape[-1])

        def part(at):
            return lax.dynamic_index_in_dim(parts, at, 1, keepdims=False)

        total = part(digit).astype(F32)
        for s in range(1, size):
            total = total + shifted(part((digit + s) % size), size, stride, s).astype(F32)
        self.held[dim] = 1
        self.value = total.astype(self.kind) if self.order else total
        return self.value

    def rest(self):
        while self.order:
            self.step()
        return self.value.reshape(self.rows, -1)


class Sum:
    def __init__(self, value, order):
        self.sizes, self.strides = split_axis(lax.axis_size(AXIS))
        self.value, self.order = value, list(order)

    def step(self):
        dim = self.order.pop(0)
        size, stride = self.sizes[dim], self.strides[dim]
        total = self.value
        for s in range(1, size):
            total = total + shifted(self.value, size, stride, s)
        self.value = total
        return total

    def rest(self):
        while self.order:
            self.step()
        return self.value


def together(*chains):
    values = lax.optimization_barrier(tuple(c.value for c in chains))
    for chain, value in zip(chains, values):
        chain.value = value


def behind(value, *chains):
    values = lax.optimization_barrier((value, *[c.value for c in chains]))
    for chain, held in zip(chains, values[1:]):
        chain.value = held


def from_behind(value, steps):
    count = lax.axis_size(AXIS)
    leading, last = (max(0, -steps), min(count, count - steps))
    return lax.ppermute(value, AXIS, [(source, source + steps) for source in range(leading, last)])


def normalize(values):
    center = values - jnp.mean(values, axis=-1, keepdims=True)
    spread = jnp.mean(center * center, axis=-1, keepdims=True)
    scale = lax.rsqrt(spread + EPSILON)
    return center * scale, scale


def norm_back(tokens, error, gain):
    normal, scale = normalize(tokens)
    scaled = error * gain
    first = jnp.mean(scaled, axis=-1, keepdims=True)
    second = jnp.mean(scaled * normal, axis=-1, keepdims=True)
    return scale * (scaled - first - normal * second), error * normal


def turn(values, table, sign):
    cosine = table[0]
    back = pltpu.roll(values, 120, 1) * table[1]
    ahead = pltpu.roll(values, 8, 1) * table[2]
    return values * cosine + sign * (back + ahead)


def qkv_body(x_ref, gain_ref, shift_ref, w_ref, b_ref, table_ref, out_ref, in_ref):
    width = x_ref.shape[1]
    normal, _ = normalize(x_ref[...].astype(F32))
    rows_in = (normal * gain_ref[...] + shift_ref[...]).astype(BF16)
    in_ref[...] = rows_in
    for j in range(0, out_ref.shape[1], 256):
        mixed = mm(rows_in, w_ref[:, j : j + 256]) + b_ref[:, j : j + 256]
        if j < 2 * width:
            for c in (0, 128):
                out_ref[:, j + c : j + c + 128] = turn(
                    mixed[:, c : c + 128], table_ref, 1.0
                ).astype(BF16)
        else:
            out_ref[:, j : j + 256] = mixed.astype(BF16)


def project(tokens, gain, shift, weight, bias, table):
    rows, width = tokens.shape
    total = 3 * width
    whole = lambda i: (0, 0)
    return pl.pallas_call(
        qkv_body,
        grid=(rows // BLOCK,),
        in_specs=[
            pl.BlockSpec((BLOCK, width), lambda i: (i, 0)),
            pl.BlockSpec((1, width), whole),
            pl.BlockSpec((1, width), whole),
            pl.BlockSpec((width, total), whole),
            pl.BlockSpec((1, total), whole),
            pl.BlockSpec((3, BLOCK, 128), lambda i: (0, i, 0)),
        ],
        out_specs=[
            pl.BlockSpec((BLOCK, total), lambda i: (i, 0)),
            pl.BlockSpec((BLOCK, width), lambda i: (i, 0)),
        ],
        out_shape=[
            jax.ShapeDtypeStruct((rows, total), BF16),
            jax.ShapeDtypeStruct((rows, width), BF16),
        ],
        compiler_params=params_of("arbitrary"),
        cost_estimate=pl.CostEstimate(
            flops=2 * rows * width * total, transcendentals=0, bytes_accessed=16 << 20
        ),
        name="qkv_project",
    )(tokens, gain, shift, weight, bias, table)


def attend_body(
    prior,
    extra,
    first_ref,
    q_ref,
    k_ref,
    v_ref,
    pk_ref,
    pv_ref,
    dc_ref,
    low_ref,
    table_ref,
    *refs,
):
    ctx_ref, dq_ref, dk_ref, dv_ref, pdk_ref, pdv_ref, keys, vals, dk_sum, dv_sum = refs[extra:]
    block = pl.program_id(1)
    lead = prior // BLOCK

    @pl.when(block == 0)
    def _():
        keys[:prior] = pk_ref[...]
        keys[prior:] = k_ref[...]
        vals[:prior] = pv_ref[...]
        vals[prior:] = v_ref[...]
        dk_sum[...] = jnp.zeros_like(dk_sum)
        dv_sum[...] = jnp.zeros_like(dv_sum)

    lane = lax.broadcasted_iota(jnp.int32, (BLOCK, 2 * HDIM), 1)
    heads = (lane < HDIM, lane >= HDIM)
    used = block + lead + 1 - first_ref[block]

    def blocks(count):
        start = (block + lead + 1 - count) * BLOCK
        query = (q_ref[...].astype(F32) * (HDIM**-0.5)).astype(BF16)
        incoming = dc_ref[...]
        low = low_ref[...]
        column = lax.broadcasted_iota(jnp.int32, (BLOCK, BLOCK), 1)
        row = lax.broadcasted_iota(jnp.int32, (BLOCK, BLOCK), 0)
        spans = [pl.ds(pl.multiple_of(start + b * BLOCK, BLOCK), BLOCK) for b in range(count)]
        ctx, d_query = [], []
        d_keys, d_vals = [[] for _ in spans], [[] for _ in spans]
        for mine in heads:
            own_query = jnp.where(mine, query, jnp.zeros_like(query))
            own_incoming = jnp.where(mine, incoming, jnp.zeros_like(incoming))
            scores = []
            for b, span in enumerate(spans):
                score = mm_bt(own_query, keys[span])
                allowed = column >= low - (start + b * BLOCK)
                if b == count - 1:
                    allowed = allowed & (column <= row)
                scores.append(jnp.where(allowed, score, MASKED))
            highest = functools.reduce(jnp.maximum, scores)
            highest = jnp.max(highest, axis=-1, keepdims=True)
            grown = [jnp.exp(score - highest) for score in scores]
            normal = jnp.sum(functools.reduce(jnp.add, grown), axis=-1, keepdims=True)
            inverse = 1.0 / normal
            probs = [g * inverse for g in grown]
            low_probs = [p.astype(BF16) for p in probs]
            d_probs = [mm_bt(own_incoming, vals[span]) for span in spans]
            inner = functools.reduce(jnp.add, [p * d for p, d in zip(probs, d_probs)])
            inner = jnp.sum(inner, axis=-1, keepdims=True)
            d_scores = [(p * (d - inner)).astype(BF16) for p, d in zip(probs, d_probs)]
            ctx.append(functools.reduce(jnp.add, [mm(p, vals[s]) for p, s in zip(low_probs, spans)]))
            d_query.append(
                functools.reduce(jnp.add, [mm(d, keys[s]) for d, s in zip(d_scores, spans)])
            )
            for b in range(count):
                d_keys[b].append(mm_at(d_scores[b], query))
                d_vals[b].append(mm_at(low_probs[b], incoming))
        ctx_ref[...] = jnp.where(heads[0], ctx[0], ctx[1]).astype(BF16)
        both = jnp.where(heads[0], d_query[0], d_query[1]) * (HDIM**-0.5)
        dq_ref[...] = turn(both, table_ref, -1.0).astype(BF16)
        for b, span in enumerate(spans):
            dk_sum[span] += jnp.where(heads[0], d_keys[b][0], d_keys[b][1])
            dv_sum[span] += jnp.where(heads[0], d_vals[b][0], d_vals[b][1])

    most = k_ref.shape[0] // BLOCK + 1
    for count in range(1, most + 1):
        pl.when(used == count)(functools.partial(blocks, count))

    @pl.when(block == pl.num_programs(1) - 1)
    def _():
        pdk_ref[...] = dk_sum[:prior].astype(BF16)
        pdv_ref[...] = dv_sum[:prior].astype(BF16)
        dk_ref[...] = dk_sum[prior:]
        dv_ref[...] = dv_sum[prior:]


def attend(first, qkv, before, d_context, low, table, begin, count, made=(), after=()):
    rows, width = d_context.shape
    prior = before.shape[0]
    pairs = width // 128
    wide = lambda off: (lambda p, i, f: (0, off + begin + p))
    tile = lambda p, i, f: (i, begin + p)
    extra = (*made, *after)
    return pl.pallas_call(
        functools.partial(attend_body, prior, len(extra)),
        grid_spec=pltpu.PrefetchScalarGridSpec(
            num_scalar_prefetch=1,
            grid=(count, rows // BLOCK),
            in_specs=[
                pl.BlockSpec((BLOCK, 128), tile),
                pl.BlockSpec((rows, 128), wide(pairs)),
                pl.BlockSpec((rows, 128), wide(2 * pairs)),
                pl.BlockSpec((prior, 128), wide(0)),
                pl.BlockSpec((prior, 128), wide(pairs)),
                pl.BlockSpec((BLOCK, 128), tile),
                pl.BlockSpec((BLOCK, 1), lambda p, i, f: (i, 0)),
                pl.BlockSpec((3, BLOCK, 128), lambda p, i, f: (0, i, 0)),
                *[pl.BlockSpec(memory_space=pl.ANY) for _ in extra],
            ],
            out_specs=[
                pl.BlockSpec((BLOCK, 128), tile),
                pl.BlockSpec((BLOCK, 128), tile),
                pl.BlockSpec((rows, 128), wide(0)),
                pl.BlockSpec((rows, 128), wide(0)),
                pl.BlockSpec((prior, 128), lambda p, i, f: (0, p)),
                pl.BlockSpec((prior, 128), lambda p, i, f: (0, p)),
            ],
            scratch_shapes=[
                pltpu.VMEM((prior + rows, 128), BF16),
                pltpu.VMEM((prior + rows, 128), BF16),
                pltpu.VMEM((prior + rows, 128), F32),
                pltpu.VMEM((prior + rows, 128), F32),
            ],
        ),
        out_shape=[
            jax.ShapeDtypeStruct((rows, width), BF16),
            jax.ShapeDtypeStruct((rows, width), BF16),
            jax.ShapeDtypeStruct((rows, width), F32),
            jax.ShapeDtypeStruct((rows, width), F32),
            jax.ShapeDtypeStruct((prior, 128 * count), BF16),
            jax.ShapeDtypeStruct((prior, 128 * count), BF16),
        ],
        compiler_params=params_of("arbitrary", "arbitrary"),
        cost_estimate=pl.CostEstimate(
            flops=8 * 10**9 * count, transcendentals=10**6 * count, bytes_accessed=4 * count << 20
        ),
        input_output_aliases={9 + i: i for i in range(len(made))},
        name="attend",
    )(first, qkv, qkv, qkv, before, before, d_context, low, table, *extra)


def mlp_body(
    x_ref,
    cot_ref,
    gain_ref,
    shift_ref,
    up_ref,
    bias_ref,
    down_ref,
    ffn_ref,
    d_up_ref,
    d_down_ref,
    d_bias_ref,
    back_ref,
    d_gain_ref,
    d_shift_ref,
    d_out_ref,
    in_ref,
    active,
    d_hidden,
):
    step = pl.program_id(0)
    rows = x_ref.shape[0]
    spans = [slice(r, r + BLOCK) for r in range(0, rows, BLOCK)]

    @pl.when(step == 0)
    def _():
        for s in spans:
            normal, _ = normalize(x_ref[s].astype(F32))
            in_ref[s] = (normal * gain_ref[...] + shift_ref[...]).astype(BF16)
        ffn_ref[...] = jnp.zeros_like(ffn_ref)
        back_ref[...] = jnp.zeros_like(back_ref)
        d_out_ref[...] = jnp.sum(cot_ref[...].astype(F32), axis=0, keepdims=True)

    summed = 0.0
    for s in spans:
        hidden = mm(in_ref[s], up_ref[...]) + bias_ref[...]
        d_active = mm_bt(cot_ref[s], down_ref[...])
        phi = 0.5 + 0.5 * lax.erf(hidden * (0.5**0.5))
        density = jnp.exp(hidden * hidden * -0.5) * 0.3989422804014327
        active[s] = (hidden * phi).astype(BF16)
        moved = (d_active * (phi + hidden * density)).astype(BF16)
        d_hidden[s] = moved
        summed = summed + jnp.sum(moved.astype(F32), axis=0, keepdims=True)
    d_bias_ref[...] = summed
    d_down_ref[...] = mm_at(active[...], cot_ref[...]).astype(BF16)
    d_up_ref[...] = mm_at(in_ref[...], d_hidden[...]).astype(BF16)
    for s in spans:
        ffn_ref[s] += mm(active[s], down_ref[...])
        back_ref[s] += mm_bt(d_hidden[s], up_ref[...])

    @pl.when(step == pl.num_programs(0) - 1)
    def _():
        d_gain, d_shift = 0.0, 0.0
        for s in spans:
            error = back_ref[s]
            moved, product = norm_back(x_ref[s].astype(F32), error, gain_ref[...])
            d_gain = d_gain + jnp.sum(product, axis=0, keepdims=True)
            d_shift = d_shift + jnp.sum(error, axis=0, keepdims=True)
            back_ref[s] = cot_ref[s].astype(F32) + moved
        d_gain_ref[...] = d_gain
        d_shift_ref[...] = d_shift


def mlp(tokens, cotangent, gain, shift, up, up_bias, down):
    rows, width = tokens.shape
    ff = down.shape[0]
    tile = 512
    whole = lambda j: (0, 0)
    vector = pl.BlockSpec((1, width), whole)
    full = pl.BlockSpec((rows, width), whole)
    return pl.pallas_call(
        mlp_body,
        grid=(ff // tile,),
        in_specs=[
            full,
            full,
            vector,
            vector,
            pl.BlockSpec((width, tile), lambda j: (0, j)),
            pl.BlockSpec((1, tile), lambda j: (0, j)),
            pl.BlockSpec((tile, width), lambda j: (j, 0)),
        ],
        out_specs=[
            full,
            pl.BlockSpec((width, tile), lambda j: (0, j)),
            pl.BlockSpec((tile, width), lambda j: (j, 0)),
            pl.BlockSpec((1, tile), lambda j: (0, j)),
            full,
            vector,
            vector,
            vector,
        ],
        out_shape=[
            jax.ShapeDtypeStruct((rows, width), F32),
            jax.ShapeDtypeStruct((width, ff), BF16),
            jax.ShapeDtypeStruct((ff, width), BF16),
            jax.ShapeDtypeStruct((1, ff), F32),
            jax.ShapeDtypeStruct((rows, width), F32),
            jax.ShapeDtypeStruct((1, width), F32),
            jax.ShapeDtypeStruct((1, width), F32),
            jax.ShapeDtypeStruct((1, width), F32),
        ],
        scratch_shapes=[
            pltpu.VMEM((rows, width), BF16),
            pltpu.VMEM((rows, tile), BF16),
            pltpu.VMEM((rows, tile), BF16),
        ],
        compiler_params=params_of("arbitrary"),
        cost_estimate=pl.CostEstimate(
            flops=12 * rows * width * ff, transcendentals=2 * rows * ff, bytes_accessed=30 << 20
        ),
        name="mlp",
    )(tokens, cotangent, gain, shift, up, up_bias, down)


def back_body(
    per_part,
    x_ref,
    in_ref,
    gain_ref,
    wq_ref,
    w_ref,
    dq_ref,
    dk_ref,
    dv_ref,
    hk_ref,
    hv_ref,
    table_ref,
    rest_ref,
    *refs,
):
    d_w_ref, d_bias_ref, grad_ref, d_gain_ref, d_shift_ref, moved = refs[-6:]
    step = pl.program_id(0)
    rows = x_ref.shape[0]
    own = rows - hk_ref.shape[0]
    spans = [slice(r, r + BLOCK) for r in range(0, rows, BLOCK)]

    @pl.when(step == 0)
    def _():
        for s in spans:
            grad_ref[s] = mm_bt(dq_ref[s], wq_ref[...])

    @pl.when(step < per_part)
    def _():
        for s in spans:
            for c in range(0, moved.shape[1], 128):
                part = dk_ref[s, c : c + 128]
                if s.start >= own:
                    part = part + hk_ref[s.start - own : s.stop - own, c : c + 128].astype(F32)
                moved[s, c : c + 128] = turn(part, table_ref[:, s], -1.0).astype(BF16)

    @pl.when(step >= per_part)
    def _():
        for s in spans:
            part = dv_ref[s]
            if s.start >= own:
                part = part + hv_ref[s.start - own : s.stop - own].astype(F32)
            moved[s] = part.astype(BF16)

    d_bias_ref[...] = jnp.sum(moved[...].astype(F32), axis=0, keepdims=True)
    d_w_ref[...] = mm_at(in_ref[...], moved[...]).astype(BF16)
    for s in spans:
        grad_ref[s] += mm_bt(moved[s], w_ref[...])


    @pl.when(step == pl.num_programs(0) - 1)
    def _():
        d_gain, d_shift = 0.0, 0.0
        for s in spans:
            error = grad_ref[s]
            back, product = norm_back(x_ref[s].astype(F32), error, gain_ref[...])
            d_gain = d_gain + jnp.sum(product, axis=0, keepdims=True)
            d_shift = d_shift + jnp.sum(error, axis=0, keepdims=True)
            grad_ref[s] = rest_ref[s] + back
        d_gain_ref[...] = d_gain
        d_shift_ref[...] = d_shift


def back(tokens, attn_in, gain, weight, dq, dk, dv, halo_k, halo_v, table, rest, after):
    rows, width = tokens.shape
    tile = 256
    per = width // tile
    prior = halo_k.shape[0]
    whole = lambda j: (0, 0)
    vector = pl.BlockSpec((1, width), whole)
    full = pl.BlockSpec((rows, width), whole)
    near = lambda off: (lambda j: (0, jnp.clip(j - off, 0, per - 1)))
    return pl.pallas_call(
        functools.partial(back_body, per),
        grid=(2 * per,),
        in_specs=[
            full,
            full,
            vector,
            pl.BlockSpec((width, width), whole),
            pl.BlockSpec((width, tile), lambda j: (0, per + j)),
            full,
            pl.BlockSpec((rows, tile), near(0)),
            pl.BlockSpec((rows, tile), near(per)),
            pl.BlockSpec((prior, tile), near(0)),
            pl.BlockSpec((prior, tile), near(per)),
            pl.BlockSpec((3, rows, 128), lambda j: (0, 0, 0)),
            full,
            *[pl.BlockSpec(memory_space=pl.ANY) for _ in after],
        ],
        out_specs=[
            pl.BlockSpec((width, tile), lambda j: (0, j)),
            pl.BlockSpec((1, tile), lambda j: (0, j)),
            full,
            vector,
            vector,
        ],
        out_shape=[
            jax.ShapeDtypeStruct((width, 2 * width), BF16),
            jax.ShapeDtypeStruct((1, 2 * width), F32),
            jax.ShapeDtypeStruct((rows, width), F32),
            jax.ShapeDtypeStruct((1, width), F32),
            jax.ShapeDtypeStruct((1, width), F32),
        ],
        scratch_shapes=[pltpu.VMEM((rows, tile), BF16)],
        compiler_params=params_of("arbitrary"),
        cost_estimate=pl.CostEstimate(
            flops=10 * rows * width * width, transcendentals=0, bytes_accessed=30 << 20
        ),
        name="qkv_back",
    )(tokens, attn_in, gain, weight, weight, dq, dk, dv, halo_k, halo_v, table, rest, *after)


def local(
    tokens,
    seq_ids,
    cotangent,
    attn_gain,
    attn_shift,
    mlp_gain,
    mlp_shift,
    qkv_weight,
    qkv_bias,
    out_weight,
    out_bias,
    up_weight,
    up_bias,
    down_weight,
    down_bias,
):
    rows, width = tokens.shape
    own = attn_gain.shape[0]
    prior = rows // 2
    vectors = (
        attn_gain,
        attn_shift,
        mlp_gain,
        mlp_shift,
        qkv_bias,
        out_bias,
        up_bias,
        down_bias,
    )
    count = lax.axis_size(AXIS)
    packed = jnp.concatenate(vectors)
    packed = jnp.pad(packed, (0, own * 128 - packed.shape[0])).reshape(own, 128)

    w_up = lax.all_gather(up_weight, AXIS, axis=0, tiled=True)
    w_down = Gather(down_weight, (0, 2, 1, 3))
    w_attn = Gather(jnp.concatenate([qkv_weight, out_weight, packed], axis=1), (0, 1, 2, 3))
    w_attn.step(), w_down.step()
    for _ in range(3):
        together(w_attn, w_down)
        w_attn.step(), w_down.step()
    w_attn, w_down = w_attn.whole(), w_down.whole()
    w_out = w_attn[:, 3 * width : 4 * width]
    small = w_attn[:, 4 * width :].reshape(count, own * 128).astype(F32)
    flat, at = [], 0
    for v in vectors:
        flat.append(small[:, at : at + v.shape[0]].reshape(1, -1))
        at += v.shape[0]
    gain_a, shift_a, gain_m, shift_m, b_qkv, b_out, b_up, b_down = flat

    row_index = jnp.arange(rows, dtype=jnp.int32)
    last_id = seq_ids[rows - 1]
    trailing = jnp.sum((seq_ids == last_id).astype(jnp.int32))
    before = from_behind(jnp.stack([last_id, trailing]), 1)
    carry = jnp.where(before[0] == seq_ids[0], before[1], 0)
    smaller = jnp.sum((seq_ids[None, :] < seq_ids[:, None]).astype(jnp.int32), axis=1)
    begins = jnp.where(seq_ids == seq_ids[0], -carry, smaller)
    low = begins + prior
    first_block = low[::BLOCK] // BLOCK
    frequency = 10000.0 ** (-2.0 * jnp.arange(ROT // 2, dtype=F32) / ROT)
    angles = (row_index - begins).astype(F32)[:, None] * frequency[None, :]
    cosine, sine = jnp.cos(angles), jnp.sin(angles)
    lane = jnp.arange(128) % HDIM
    spread = lambda v: jnp.tile(v, (1, 128 // v.shape[1]))
    table = jnp.stack(
        [
            jnp.where(lane < ROT, spread(cosine), 1.0),
            jnp.where(lane < ROT // 2, -spread(sine), 0.0),
            jnp.where((lane >= ROT // 2) & (lane < ROT), spread(sine), 0.0),
        ]
    )

    qkv, attn_in = project(tokens, gain_a, shift_a, w_attn, b_qkv, table)
    halo = from_behind(qkv[rows - prior :, width:], 1)
    ffn, d_up, d_down, d_up_bias, rest, d_gain_m, d_shift_m, d_out_bias = mlp(
        tokens, cotangent, gain_m, shift_m, w_up, b_up, w_down
    )
    d_up = lax.psum_scatter(d_up, AXIS, scatter_dimension=0, tiled=True).astype(F32)
    d_down = Scatter(d_down, (3, 1, 2, 0))
    d_context = mm_bt(cotangent, w_out).astype(BF16)
    pairs = width // 128
    context, dq, dk, dv, back_k, back_v = attend(
        first_block, qkv, halo, d_context, low[:, None], table, 0, pairs
    )
    halo_k, halo_v = from_behind(back_k, -1), from_behind(back_v, -1)
    d_down.step()
    d_outq = jnp.concatenate(
        [mm_at(context, cotangent).astype(BF16), mm_at(attn_in, dq).astype(BF16)], axis=1
    )
    d_outq = Scatter(d_outq, (3, 2, 1, 0))
    d_bias_q = jnp.sum(dq.astype(F32), axis=0, keepdims=True)
    block_out = (tokens.astype(F32) + (mm(context, w_out) + b_out) + (ffn + b_down)).astype(BF16)
    d_outq.step()
    behind((halo_k, halo_v), d_outq)
    summed = (d_down.step(),)
    d_wkv, d_bias_kv, grad_tokens, d_gain_a, d_shift_a = back(
        tokens, attn_in, gain_a, w_attn, dq, dk, dv, halo_k, halo_v, table, rest, summed
    )

    d_wkv = Scatter(d_wkv, (3, 1, 2, 0))
    d_down.step(), d_outq.step()
    together(d_down, d_outq, d_wkv)
    sums = (
        d_gain_a,
        d_shift_a,
        d_gain_m,
        d_shift_m,
        d_bias_q,
        d_bias_kv,
        d_out_bias,
        d_up_bias,
    )
    wide = Sum(jnp.concatenate([s.reshape(-1, 128) for s in sums], axis=0), (3, 2, 1, 0))
    for at in range(3):
        chains = [c for c in (d_wkv, wide, d_outq, d_down) if c.order]
        for chain in chains:
            chain.step()
        chains = [c for c in chains if c.order]
        together(*chains)
    wide = wide.rest().reshape(-1)
    me = lax.axis_index(AXIS)
    out, at = [], 0
    for many in (1, 1, 1, 1, 3, 1, 4):
        out.append(lax.dynamic_slice_in_dim(wide, at + me * many * own, many * own))
        at += many * width
    g_gain_a, g_shift_a, g_gain_m, g_shift_m, g_qkv_b, g_out_b, g_up_b = out
    d_outq, d_wkv, d_down = d_outq.rest(), d_wkv.rest(), d_down.rest()
    d_out = d_outq[:, :width]
    d_qkv = jnp.concatenate([d_outq[:, width:], d_wkv], axis=1)
    return (
        block_out,
        grad_tokens,
        g_gain_a,
        g_shift_a,
        g_gain_m,
        g_shift_m,
        d_qkv,
        g_qkv_b,
        d_out,
        g_out_b,
        d_up,
        g_up_b,
        d_down,
        g_out_b,
    )


def solution(mesh):
    wide, thin = P("dev", None), P("dev")
    return jax.shard_map(
        local,
        mesh=mesh,
        in_specs=(
            wide,
            thin,
            wide,
            thin,
            thin,
            thin,
            thin,
            wide,
            thin,
            wide,
            thin,
            wide,
            thin,
            wide,
            thin,
        ),
        out_specs=(
            wide,
            wide,
            thin,
            thin,
            thin,
            thin,
            wide,
            thin,
            wide,
            thin,
            wide,
            thin,
            wide,
            thin,
        ),
        check_vma=False,
    )
```

```python
import functools

import jax
import jax.numpy as jnp
from jax import lax
from jax.experimental import pallas as pl
from jax.experimental.pallas import tpu as pltpu
from jax.sharding import PartitionSpec as P

HDIM = 64
ROT = 16
EPSILON = 1e-05
MASKED = -1e30
BLOCK = 256
VMEM_BYTES = 58 << 20
F32 = jnp.float32
BF16 = jnp.bfloat16
AXIS = "dev"


def params_of(*semantics):
    return pltpu.CompilerParams(dimension_semantics=semantics, vmem_limit_bytes=VMEM_BYTES)


def mm(a, b):
    return lax.dot_general(a, b, (((1,), (0,)), ((), ())), preferred_element_type=F32)


def mm_bt(a, b):
    return lax.dot_general(a, b, (((1,), (1,)), ((), ())), preferred_element_type=F32)


def mm_at(a, b):
    return lax.dot_general(a, b, (((0,), (0,)), ((), ())), preferred_element_type=F32)


def split_axis(count):
    bits = (count // 2).bit_length() - 1
    small = 1 << (bits // 3)
    sizes = [count // 2 // small // small, small, small, 2]
    strides = [small * small * 2, small * 2, 2, 1]
    return sizes, strides


def shifted(value, size, stride, steps):
    count = lax.axis_size(AXIS)
    moves = []
    for source in range(count):
        digit = source // stride % size
        moves.append((source, source + ((digit + steps) % size - digit) * stride))
    return lax.ppermute(value, AXIS, moves)


def place(pieces, digit):
    count = len(pieces)
    if count == 2:
        mine, other = pieces
        first = jnp.where(digit == 0, mine, other)
        second = jnp.where(digit == 0, other, mine)
        return jnp.stack([first, second], axis=1)
    slots = [pieces[0]] * count
    for j in range(count):
        slots[j] = lax.select_n((digit - j) % count, *pieces)
    return jnp.stack(slots, axis=1)


class Gather:
    def __init__(self, value, order):
        self.sizes, self.strides = split_axis(lax.axis_size(AXIS))
        self.value, self.order = value, list(order)
        self.rows, self.width = value.shape
        self.held = [1, 1, 1, 1]

    def step(self):
        dim = self.order.pop(0)
        size, stride = self.sizes[dim], self.strides[dim]
        digit = lax.axis_index(AXIS) // stride % size
        outer, inner = 1, self.rows
        for d in range(4):
            if d < dim:
                outer *= self.held[d]
            if d > dim:
                inner *= self.held[d]
        piece = self.value.reshape(outer, inner, self.width)
        pieces = [piece] + [shifted(piece, size, stride, s) for s in range(1, size)]
        self.value = place(pieces, digit)
        self.held[dim] = size

    def whole(self):
        return self.value.reshape(lax.axis_size(AXIS) * self.rows, self.width)


class Scatter:
    def __init__(self, value, order):
        self.sizes, self.strides = split_axis(lax.axis_size(AXIS))
        self.value, self.order, self.kind = value, list(order), value.dtype
        self.rows = value.shape[0] // lax.axis_size(AXIS)
        self.held = list(self.sizes)

    def step(self):
        dim = self.order.pop(0)
        size, stride = self.sizes[dim], self.strides[dim]
        digit = lax.axis_index(AXIS) // stride % size
        outer, inner = 1, self.rows
        for d in range(4):
            if d < dim:
                outer *= self.held[d]
            if d > dim:
                inner *= self.held[d]
        parts = self.value.reshape(outer, size, inner, self.value.shape[-1])

        def part(at):
            return lax.dynamic_index_in_dim(parts, at, 1, keepdims=False)

        total = part(digit).astype(F32)
        for s in range(1, size):
            total = total + shifted(part((digit + s) % size), size, stride, s).astype(F32)
        self.held[dim] = 1
        self.value = total.astype(self.kind) if self.order else total
        return self.value

    def rest(self):
        while self.order:
            self.step()
        return self.value.reshape(self.rows, -1)


class Sum:
    def __init__(self, value, order):
        self.sizes, self.strides = split_axis(lax.axis_size(AXIS))
        self.value, self.order = value, list(order)

    def step(self):
        dim = self.order.pop(0)
        size, stride = self.sizes[dim], self.strides[dim]
        total = self.value
        for s in range(1, size):
            total = total + shifted(self.value, size, stride, s)
        self.value = total
        return total

    def rest(self):
        while self.order:
            self.step()
        return self.value


def together(*chains):
    values = lax.optimization_barrier(tuple(c.value for c in chains))
    for chain, value in zip(chains, values):
        chain.value = value


def behind(value, *chains):
    values = lax.optimization_barrier((value, *[c.value for c in chains]))
    for chain, held in zip(chains, values[1:]):
        chain.value = held


def from_behind(value, steps):
    count = lax.axis_size(AXIS)
    leading, last = (max(0, -steps), min(count, count - steps))
    return lax.ppermute(value, AXIS, [(source, source + steps) for source in range(leading, last)])


def normalize(values):
    center = values - jnp.mean(values, axis=-1, keepdims=True)
    spread = jnp.mean(center * center, axis=-1, keepdims=True)
    scale = lax.rsqrt(spread + EPSILON)
    return center * scale, scale


def norm_back(tokens, error, gain):
    normal, scale = normalize(tokens)
    scaled = error * gain
    first = jnp.mean(scaled, axis=-1, keepdims=True)
    second = jnp.mean(scaled * normal, axis=-1, keepdims=True)
    return scale * (scaled - first - normal * second), error * normal


def turn(values, table, sign):
    cosine = table[0]
    back = pltpu.roll(values, 120, 1) * table[1]
    ahead = pltpu.roll(values, 8, 1) * table[2]
    return values * cosine + sign * (back + ahead)


def qkv_body(x_ref, gain_ref, shift_ref, w_ref, b_ref, table_ref, out_ref, in_ref):
    width = x_ref.shape[1]
    normal, _ = normalize(x_ref[...].astype(F32))
    rows_in = (normal * gain_ref[...] + shift_ref[...]).astype(BF16)
    in_ref[...] = rows_in
    for j in range(0, out_ref.shape[1], 256):
        mixed = mm(rows_in, w_ref[:, j : j + 256]) + b_ref[:, j : j + 256]
        if j < 2 * width:
            for c in (0, 128):
                out_ref[:, j + c : j + c + 128] = turn(
                    mixed[:, c : c + 128], table_ref, 1.0
                ).astype(BF16)
        else:
            out_ref[:, j : j + 256] = mixed.astype(BF16)


def project(tokens, gain, shift, weight, bias, table):
    rows, width = tokens.shape
    total = 3 * width
    whole = lambda i: (0, 0)
    return pl.pallas_call(
        qkv_body,
        grid=(rows // BLOCK,),
        in_specs=[
            pl.BlockSpec((BLOCK, width), lambda i: (i, 0)),
            pl.BlockSpec((1, width), whole),
            pl.BlockSpec((1, width), whole),
            pl.BlockSpec((width, total), whole),
            pl.BlockSpec((1, total), whole),
            pl.BlockSpec((3, BLOCK, 128), lambda i: (0, i, 0)),
        ],
        out_specs=[
            pl.BlockSpec((BLOCK, total), lambda i: (i, 0)),
            pl.BlockSpec((BLOCK, width), lambda i: (i, 0)),
        ],
        out_shape=[
            jax.ShapeDtypeStruct((rows, total), BF16),
            jax.ShapeDtypeStruct((rows, width), BF16),
        ],
        compiler_params=params_of("arbitrary"),
        cost_estimate=pl.CostEstimate(
            flops=2 * rows * width * total, transcendentals=0, bytes_accessed=16 << 20
        ),
        name="qkv_project",
    )(tokens, gain, shift, weight, bias, table)


def attend_body(
    prior,
    extra,
    first_ref,
    q_ref,
    k_ref,
    v_ref,
    pk_ref,
    pv_ref,
    dc_ref,
    low_ref,
    table_ref,
    *refs,
):
    ctx_ref, dq_ref, dk_ref, dv_ref, pdk_ref, pdv_ref, keys, vals, dk_sum, dv_sum = refs[extra:]
    block = pl.program_id(1)
    lead = prior // BLOCK

    @pl.when(block == 0)
    def _():
        keys[:prior] = pk_ref[...]
        keys[prior:] = k_ref[...]
        vals[:prior] = pv_ref[...]
        vals[prior:] = v_ref[...]
        dk_sum[...] = jnp.zeros_like(dk_sum)
        dv_sum[...] = jnp.zeros_like(dv_sum)

    lane = lax.broadcasted_iota(jnp.int32, (BLOCK, 2 * HDIM), 1)
    heads = (lane < HDIM, lane >= HDIM)
    used = block + lead + 1 - first_ref[block]

    def blocks(count):
        start = (block + lead + 1 - count) * BLOCK
        query = (q_ref[...].astype(F32) * (HDIM**-0.5)).astype(BF16)
        incoming = dc_ref[...]
        low = low_ref[...]
        column = lax.broadcasted_iota(jnp.int32, (BLOCK, BLOCK), 1)
        row = lax.broadcasted_iota(jnp.int32, (BLOCK, BLOCK), 0)
        spans = [pl.ds(pl.multiple_of(start + b * BLOCK, BLOCK), BLOCK) for b in range(count)]
        ctx, d_query = [], []
        d_keys, d_vals = [[] for _ in spans], [[] for _ in spans]
        for mine in heads:
            own_query = jnp.where(mine, query, jnp.zeros_like(query))
            own_incoming = jnp.where(mine, incoming, jnp.zeros_like(incoming))
            scores = []
            for b, span in enumerate(spans):
                score = mm_bt(own_query, keys[span])
                allowed = column >= low - (start + b * BLOCK)
                if b == count - 1:
                    allowed = allowed & (column <= row)
                scores.append(jnp.where(allowed, score, MASKED))
            highest = functools.reduce(jnp.maximum, scores)
            highest = jnp.max(highest, axis=-1, keepdims=True)
            grown = [jnp.exp(score - highest) for score in scores]
            normal = jnp.sum(functools.reduce(jnp.add, grown), axis=-1, keepdims=True)
            inverse = 1.0 / normal
            probs = [g * inverse for g in grown]
            low_probs = [p.astype(BF16) for p in probs]
            d_probs = [mm_bt(own_incoming, vals[span]) for span in spans]
            inner = functools.reduce(jnp.add, [p * d for p, d in zip(probs, d_probs)])
            inner = jnp.sum(inner, axis=-1, keepdims=True)
            d_scores = [(p * (d - inner)).astype(BF16) for p, d in zip(probs, d_probs)]
            ctx.append(functools.reduce(jnp.add, [mm(p, vals[s]) for p, s in zip(low_probs, spans)]))
            d_query.append(
                functools.reduce(jnp.add, [mm(d, keys[s]) for d, s in zip(d_scores, spans)])
            )
            for b in range(count):
                d_keys[b].append(mm_at(d_scores[b], query))
                d_vals[b].append(mm_at(low_probs[b], incoming))
        ctx_ref[...] = jnp.where(heads[0], ctx[0], ctx[1]).astype(BF16)
        both = jnp.where(heads[0], d_query[0], d_query[1]) * (HDIM**-0.5)
        dq_ref[...] = turn(both, table_ref, -1.0).astype(BF16)
        for b, span in enumerate(spans):
            dk_sum[span] += jnp.where(heads[0], d_keys[b][0], d_keys[b][1])
            dv_sum[span] += jnp.where(heads[0], d_vals[b][0], d_vals[b][1])

    most = k_ref.shape[0] // BLOCK + 1
    for count in range(1, most + 1):
        pl.when(used == count)(functools.partial(blocks, count))

    @pl.when(block == pl.num_programs(1) - 1)
    def _():
        pdk_ref[...] = dk_sum[:prior].astype(BF16)
        pdv_ref[...] = dv_sum[:prior].astype(BF16)
        dk_ref[...] = dk_sum[prior:]
        dv_ref[...] = dv_sum[prior:]


def attend(first, qkv, before, d_context, low, table, begin, count, made=(), after=()):
    rows, width = d_context.shape
    prior = before.shape[0]
    pairs = width // 128
    wide = lambda off: (lambda p, i, f: (0, off + begin + p))
    tile = lambda p, i, f: (i, begin + p)
    extra = (*made, *after)
    return pl.pallas_call(
        functools.partial(attend_body, prior, len(extra)),
        grid_spec=pltpu.PrefetchScalarGridSpec(
            num_scalar_prefetch=1,
            grid=(count, rows // BLOCK),
            in_specs=[
                pl.BlockSpec((BLOCK, 128), tile),
                pl.BlockSpec((rows, 128), wide(pairs)),
                pl.BlockSpec((rows, 128), wide(2 * pairs)),
                pl.BlockSpec((prior, 128), wide(0)),
                pl.BlockSpec((prior, 128), wide(pairs)),
                pl.BlockSpec((BLOCK, 128), tile),
                pl.BlockSpec((BLOCK, 1), lambda p, i, f: (i, 0)),
                pl.BlockSpec((3, BLOCK, 128), lambda p, i, f: (0, i, 0)),
                *[pl.BlockSpec(memory_space=pl.ANY) for _ in extra],
            ],
            out_specs=[
                pl.BlockSpec((BLOCK, 128), tile),
                pl.BlockSpec((BLOCK, 128), tile),
                pl.BlockSpec((rows, 128), wide(0)),
                pl.BlockSpec((rows, 128), wide(0)),
                pl.BlockSpec((prior, 128), lambda p, i, f: (0, p)),
                pl.BlockSpec((prior, 128), lambda p, i, f: (0, p)),
            ],
            scratch_shapes=[
                pltpu.VMEM((prior + rows, 128), BF16),
                pltpu.VMEM((prior + rows, 128), BF16),
                pltpu.VMEM((prior + rows, 128), F32),
                pltpu.VMEM((prior + rows, 128), F32),
            ],
        ),
        out_shape=[
            jax.ShapeDtypeStruct((rows, width), BF16),
            jax.ShapeDtypeStruct((rows, width), BF16),
            jax.ShapeDtypeStruct((rows, width), F32),
            jax.ShapeDtypeStruct((rows, width), F32),
            jax.ShapeDtypeStruct((prior, 128 * count), BF16),
            jax.ShapeDtypeStruct((prior, 128 * count), BF16),
        ],
        compiler_params=params_of("arbitrary", "arbitrary"),
        cost_estimate=pl.CostEstimate(
            flops=8 * 10**9 * count, transcendentals=10**6 * count, bytes_accessed=4 * count << 20
        ),
        input_output_aliases={9 + i: i for i in range(len(made))},
        name="attend",
    )(first, qkv, qkv, qkv, before, before, d_context, low, table, *extra)


def mlp_body(
    x_ref,
    cot_ref,
    gain_ref,
    shift_ref,
    up_ref,
    bias_ref,
    down_ref,
    ffn_ref,
    d_up_ref,
    d_down_ref,
    d_bias_ref,
    back_ref,
    d_gain_ref,
    d_shift_ref,
    d_out_ref,
    in_ref,
    active,
    d_hidden,
):
    step = pl.program_id(0)
    rows = x_ref.shape[0]
    spans = [slice(r, r + BLOCK) for r in range(0, rows, BLOCK)]

    @pl.when(step == 0)
    def _():
        for s in spans:
            normal, _ = normalize(x_ref[s].astype(F32))
            in_ref[s] = (normal * gain_ref[...] + shift_ref[...]).astype(BF16)
        ffn_ref[...] = jnp.zeros_like(ffn_ref)
        back_ref[...] = jnp.zeros_like(back_ref)
        d_out_ref[...] = jnp.sum(cot_ref[...].astype(F32), axis=0, keepdims=True)

    summed = 0.0
    for s in spans:
        hidden = mm(in_ref[s], up_ref[...]) + bias_ref[...]
        d_active = mm_bt(cot_ref[s], down_ref[...])
        phi = 0.5 + 0.5 * lax.erf(hidden * (0.5**0.5))
        density = jnp.exp(hidden * hidden * -0.5) * 0.3989422804014327
        active[s] = (hidden * phi).astype(BF16)
        moved = (d_active * (phi + hidden * density)).astype(BF16)
        d_hidden[s] = moved
        summed = summed + jnp.sum(moved.astype(F32), axis=0, keepdims=True)
    d_bias_ref[...] = summed
    d_down_ref[...] = mm_at(active[...], cot_ref[...]).astype(BF16)
    d_up_ref[...] = mm_at(in_ref[...], d_hidden[...]).astype(BF16)
    for s in spans:
        ffn_ref[s] += mm(active[s], down_ref[...])
        back_ref[s] += mm_bt(d_hidden[s], up_ref[...])

    @pl.when(step == pl.num_programs(0) - 1)
    def _():
        d_gain, d_shift = 0.0, 0.0
        for s in spans:
            error = back_ref[s]
            moved, product = norm_back(x_ref[s].astype(F32), error, gain_ref[...])
            d_gain = d_gain + jnp.sum(product, axis=0, keepdims=True)
            d_shift = d_shift + jnp.sum(error, axis=0, keepdims=True)
            back_ref[s] = cot_ref[s].astype(F32) + moved
        d_gain_ref[...] = d_gain
        d_shift_ref[...] = d_shift


def mlp(tokens, cotangent, gain, shift, up, up_bias, down):
    rows, width = tokens.shape
    ff = down.shape[0]
    tile = 512
    whole = lambda j: (0, 0)
    vector = pl.BlockSpec((1, width), whole)
    full = pl.BlockSpec((rows, width), whole)
    return pl.pallas_call(
        mlp_body,
        grid=(ff // tile,),
        in_specs=[
            full,
            full,
            vector,
            vector,
            pl.BlockSpec((width, tile), lambda j: (0, j)),
            pl.BlockSpec((1, tile), lambda j: (0, j)),
            pl.BlockSpec((tile, width), lambda j: (j, 0)),
        ],
        out_specs=[
            full,
            pl.BlockSpec((width, tile), lambda j: (0, j)),
            pl.BlockSpec((tile, width), lambda j: (j, 0)),
            pl.BlockSpec((1, tile), lambda j: (0, j)),
            full,
            vector,
            vector,
            vector,
        ],
        out_shape=[
            jax.ShapeDtypeStruct((rows, width), F32),
            jax.ShapeDtypeStruct((width, ff), BF16),
            jax.ShapeDtypeStruct((ff, width), BF16),
            jax.ShapeDtypeStruct((1, ff), F32),
            jax.ShapeDtypeStruct((rows, width), F32),
            jax.ShapeDtypeStruct((1, width), F32),
            jax.ShapeDtypeStruct((1, width), F32),
            jax.ShapeDtypeStruct((1, width), F32),
        ],
        scratch_shapes=[
            pltpu.VMEM((rows, width), BF16),
            pltpu.VMEM((rows, tile), BF16),
            pltpu.VMEM((rows, tile), BF16),
        ],
        compiler_params=params_of("arbitrary"),
        cost_estimate=pl.CostEstimate(
            flops=12 * rows * width * ff, transcendentals=2 * rows * ff, bytes_accessed=30 << 20
        ),
        name="mlp",
    )(tokens, cotangent, gain, shift, up, up_bias, down)


def back_body(
    per_part,
    x_ref,
    in_ref,
    gain_ref,
    wq_ref,
    w_ref,
    dq_ref,
    dk_ref,
    dv_ref,
    hk_ref,
    hv_ref,
    table_ref,
    rest_ref,
    *refs,
):
    d_w_ref, d_bias_ref, grad_ref, d_gain_ref, d_shift_ref, moved = refs[-6:]
    step = pl.program_id(0)
    rows = x_ref.shape[0]
    own = rows - hk_ref.shape[0]
    spans = [slice(r, r + BLOCK) for r in range(0, rows, BLOCK)]

    @pl.when(step == 0)
    def _():
        for s in spans:
            grad_ref[s] = mm_bt(dq_ref[s], wq_ref[...])

    @pl.when(step < per_part)
    def _():
        for s in spans:
            for c in range(0, moved.shape[1], 128):
                part = dk_ref[s, c : c + 128]
                if s.start >= own:
                    part = part + hk_ref[s.start - own : s.stop - own, c : c + 128].astype(F32)
                moved[s, c : c + 128] = turn(part, table_ref[:, s], -1.0).astype(BF16)

    @pl.when(step >= per_part)
    def _():
        for s in spans:
            part = dv_ref[s]
            if s.start >= own:
                part = part + hv_ref[s.start - own : s.stop - own].astype(F32)
            moved[s] = part.astype(BF16)

    d_bias_ref[...] = jnp.sum(moved[...].astype(F32), axis=0, keepdims=True)
    d_w_ref[...] = mm_at(in_ref[...], moved[...]).astype(BF16)
    for s in spans:
        grad_ref[s] += mm_bt(moved[s], w_ref[...])


    @pl.when(step == pl.num_programs(0) - 1)
    def _():
        d_gain, d_shift = 0.0, 0.0
        for s in spans:
            error = grad_ref[s]
            back, product = norm_back(x_ref[s].astype(F32), error, gain_ref[...])
            d_gain = d_gain + jnp.sum(product, axis=0, keepdims=True)
            d_shift = d_shift + jnp.sum(error, axis=0, keepdims=True)
            grad_ref[s] = rest_ref[s] + back
        d_gain_ref[...] = d_gain
        d_shift_ref[...] = d_shift


def back(tokens, attn_in, gain, weight, dq, dk, dv, halo_k, halo_v, table, rest, after):
    rows, width = tokens.shape
    tile = 256
    per = width // tile
    prior = halo_k.shape[0]
    whole = lambda j: (0, 0)
    vector = pl.BlockSpec((1, width), whole)
    full = pl.BlockSpec((rows, width), whole)
    near = lambda off: (lambda j: (0, jnp.clip(j - off, 0, per - 1)))
    return pl.pallas_call(
        functools.partial(back_body, per),
        grid=(2 * per,),
        in_specs=[
            full,
            full,
            vector,
            pl.BlockSpec((width, width), whole),
            pl.BlockSpec((width, tile), lambda j: (0, per + j)),
            full,
            pl.BlockSpec((rows, tile), near(0)),
            pl.BlockSpec((rows, tile), near(per)),
            pl.BlockSpec((prior, tile), near(0)),
            pl.BlockSpec((prior, tile), near(per)),
            pl.BlockSpec((3, rows, 128), lambda j: (0, 0, 0)),
            full,
            *[pl.BlockSpec(memory_space=pl.ANY) for _ in after],
        ],
        out_specs=[
            pl.BlockSpec((width, tile), lambda j: (0, j)),
            pl.BlockSpec((1, tile), lambda j: (0, j)),
            full,
            vector,
            vector,
        ],
        out_shape=[
            jax.ShapeDtypeStruct((width, 2 * width), BF16),
            jax.ShapeDtypeStruct((1, 2 * width), F32),
            jax.ShapeDtypeStruct((rows, width), F32),
            jax.ShapeDtypeStruct((1, width), F32),
            jax.ShapeDtypeStruct((1, width), F32),
        ],
        scratch_shapes=[pltpu.VMEM((rows, tile), BF16)],
        compiler_params=params_of("arbitrary"),
        cost_estimate=pl.CostEstimate(
            flops=10 * rows * width * width, transcendentals=0, bytes_accessed=30 << 20
        ),
        name="qkv_back",
    )(tokens, attn_in, gain, weight, weight, dq, dk, dv, halo_k, halo_v, table, rest, *after)


def local(
    tokens,
    seq_ids,
    cotangent,
    attn_gain,
    attn_shift,
    mlp_gain,
    mlp_shift,
    qkv_weight,
    qkv_bias,
    out_weight,
    out_bias,
    up_weight,
    up_bias,
    down_weight,
    down_bias,
):
    rows, width = tokens.shape
    own = attn_gain.shape[0]
    prior = rows // 2
    vectors = (
        attn_gain,
        attn_shift,
        mlp_gain,
        mlp_shift,
        qkv_bias,
        out_bias,
        up_bias,
        down_bias,
    )
    count = lax.axis_size(AXIS)
    packed = jnp.concatenate(vectors)
    packed = jnp.pad(packed, (0, own * 128 - packed.shape[0])).reshape(own, 128)

    w_up = lax.all_gather(up_weight, AXIS, axis=0, tiled=True)
    w_down = Gather(down_weight, (0, 2, 1, 3))
    w_attn = Gather(jnp.concatenate([qkv_weight, out_weight, packed], axis=1), (0, 1, 2, 3))
    w_attn.step(), w_down.step()
    for at in range(3):
        together(w_attn, w_down)
        if at == 2:
            behind(w_up, w_attn, w_down)
        w_attn.step(), w_down.step()
    w_attn, w_down = w_attn.whole(), w_down.whole()
    w_out = w_attn[:, 3 * width : 4 * width]
    small = w_attn[:, 4 * width :].reshape(count, own * 128).astype(F32)
    flat, at = [], 0
    for v in vectors:
        flat.append(small[:, at : at + v.shape[0]].reshape(1, -1))
        at += v.shape[0]
    gain_a, shift_a, gain_m, shift_m, b_qkv, b_out, b_up, b_down = flat

    row_index = jnp.arange(rows, dtype=jnp.int32)
    last_id = seq_ids[rows - 1]
    trailing = jnp.sum((seq_ids == last_id).astype(jnp.int32))
    before = from_behind(jnp.stack([last_id, trailing]), 1)
    carry = jnp.where(before[0] == seq_ids[0], before[1], 0)
    smaller = jnp.sum((seq_ids[None, :] < seq_ids[:, None]).astype(jnp.int32), axis=1)
    begins = jnp.where(seq_ids == seq_ids[0], -carry, smaller)
    low = begins + prior
    first_block = low[::BLOCK] // BLOCK
    frequency = 10000.0 ** (-2.0 * jnp.arange(ROT // 2, dtype=F32) / ROT)
    angles = (row_index - begins).astype(F32)[:, None] * frequency[None, :]
    cosine, sine = jnp.cos(angles), jnp.sin(angles)
    lane = jnp.arange(128) % HDIM
    spread = lambda v: jnp.tile(v, (1, 128 // v.shape[1]))
    table = jnp.stack(
        [
            jnp.where(lane < ROT, spread(cosine), 1.0),
            jnp.where(lane < ROT // 2, -spread(sine), 0.0),
            jnp.where((lane >= ROT // 2) & (lane < ROT), spread(sine), 0.0),
        ]
    )

    qkv, attn_in = project(tokens, gain_a, shift_a, w_attn, b_qkv, table)
    halo = from_behind(qkv[rows - prior :, width:], 1)
    ffn, d_up, d_down, d_up_bias, rest, d_gain_m, d_shift_m, d_out_bias = mlp(
        tokens, cotangent, gain_m, shift_m, w_up, b_up, w_down
    )
    d_up = lax.psum_scatter(d_up, AXIS, scatter_dimension=0, tiled=True).astype(F32)
    d_down = Scatter(d_down, (3, 1, 2, 0))
    d_context = mm_bt(cotangent, w_out).astype(BF16)
    pairs = width // 128
    context, dq, dk, dv, back_k, back_v = attend(
        first_block, qkv, halo, d_context, low[:, None], table, 0, pairs
    )
    halo_k, halo_v = from_behind(back_k, -1), from_behind(back_v, -1)
    d_down.step()
    d_outq = jnp.concatenate(
        [mm_at(context, cotangent).astype(BF16), mm_at(attn_in, dq).astype(BF16)], axis=1
    )
    d_outq = Scatter(d_outq, (3, 2, 1, 0))
    d_bias_q = jnp.sum(dq.astype(F32), axis=0, keepdims=True)
    block_out = (tokens.astype(F32) + (mm(context, w_out) + b_out) + (ffn + b_down)).astype(BF16)
    d_outq.step()
    behind((halo_k, halo_v), d_outq)
    summed = (d_down.step(), d_up)
    d_wkv, d_bias_kv, grad_tokens, d_gain_a, d_shift_a = back(
        tokens, attn_in, gain_a, w_attn, dq, dk, dv, halo_k, halo_v, table, rest, summed
    )

    d_wkv = Scatter(d_wkv, (3, 1, 2, 0))
    d_down.step(), d_outq.step()
    together(d_down, d_outq, d_wkv)
    sums = (
        d_gain_a,
        d_shift_a,
        d_gain_m,
        d_shift_m,
        d_bias_q,
        d_bias_kv,
        d_out_bias,
        d_up_bias,
    )
    wide = Sum(jnp.concatenate([s.reshape(-1, 128) for s in sums], axis=0), (3, 2, 1, 0))
    for at in range(3):
        chains = [c for c in (d_wkv, wide, d_outq, d_down) if c.order]
        for chain in chains:
            chain.step()
        chains = [c for c in chains if c.order]
        together(*chains)
    wide = wide.rest().reshape(-1)
    me = lax.axis_index(AXIS)
    out, at = [], 0
    for many in (1, 1, 1, 1, 3, 1, 4):
        out.append(lax.dynamic_slice_in_dim(wide, at + me * many * own, many * own))
        at += many * width
    g_gain_a, g_shift_a, g_gain_m, g_shift_m, g_qkv_b, g_out_b, g_up_b = out
    d_outq, d_wkv, d_down = d_outq.rest(), d_wkv.rest(), d_down.rest()
    d_out = d_outq[:, :width]
    d_qkv = jnp.concatenate([d_outq[:, width:], d_wkv], axis=1)
    return (
        block_out,
        grad_tokens,
        g_gain_a,
        g_shift_a,
        g_gain_m,
        g_shift_m,
        d_qkv,
        g_qkv_b,
        d_out,
        g_out_b,
        d_up,
        g_up_b,
        d_down,
        g_out_b,
    )


def solution(mesh):
    wide, thin = P("dev", None), P("dev")
    return jax.shard_map(
        local,
        mesh=mesh,
        in_specs=(
            wide,
            thin,
            wide,
            thin,
            thin,
            thin,
            thin,
            wide,
            thin,
            wide,
            thin,
            wide,
            thin,
            wide,
            thin,
        ),
        out_specs=(
            wide,
            wide,
            thin,
            thin,
            thin,
            thin,
            wide,
            thin,
            wide,
            thin,
            wide,
            thin,
            wide,
            thin,
        ),
        check_vma=False,
    )
```
